256 devices in a mesh: dp: 32 (over y, z_hi, core), factor: 8 (over z_lo, x).
Axes of the slice: x: 4, y: 4, z: 8 (z_hi: 4, z_lo: 2; z = z_hi * 2 + z_lo), core: 2. Of those that a mesh axis runs over, the one named last changes fastest.
Arguments:
- grad_out: bfloat16 [32, 128, 14336], P('dp', None, 'factor'), may hold values from -6 to 6
- act_in: bfloat16 [32, 128, 4096], P('dp', None, 'factor'), may hold values from -6 to 6
- basis_out: bfloat16 [14336, 14336], P('factor', 'dp'), may hold values from -0.046875 to 0.046875
- basis_in: bfloat16 [4096, 4096], P('factor', 'dp'), may hold values from -0.09375 to 0.09375
- eigen_vals: bfloat16 [14336, 4096], P('dp'), may hold values from 0.25 to 4
- query_out: bfloat16 [16, 8, 14336], P(None, None, 'factor'), may hold values from -0.01171875 to 0.01171875
- query_in: bfloat16 [16, 8, 4096], P(None, None, 'factor'), may hold values from -0.01171875 to 0.01171875
Outputs:
- scores: float32 [32, 16], P('factor')
The draws below stay inside these ranges and needn't reach their ends.
All inputs are finite; a program needn't handle non-finite values.
Results may differ from the reference program's by a relative error of at most 0.023.
Values may be sent and summed in bfloat16 or wider, within the bound.
No kernel may reach another device: no remote copies, remote signals or barrier semaphores. Data moves between devices by JAX's collectives and lax.ppermute only.
A program may use at most 128 MiB of HBM per device.

```python
import math
import jax
import jax.numpy as jnp
from jax import lax

D = 4096
FF = 14336
RANK = 8
TOKENS = 128
QUERIES = 16
SEQS = 32
N_FACTOR = 8


def block_scale(own_key, extent, shards, smallest, high):
    factor_of, own = 1.0, jax.random.fold_in(own_key, 6)
    for dim, parts in shards:
        heights = jnp.exp(jax.random.uniform(jax.random.fold_in(own, dim), (parts,), jnp.float32, smallest / len(shards), high / len(shards)))
        factor_of = factor_of * jnp.repeat(heights, extent[dim] // parts).reshape([-1 if axis == dim else 1 for axis in range(len(extent))])
    return factor_of


def normal_values(stream_key, dims, scale, most, pieces=(), dtype=jnp.bfloat16):
    array = scale * jax.random.normal(stream_key, dims, jnp.float32)
    if pieces:
        array = array * block_scale(stream_key, dims, pieces, -0.22, 0.18)
    return jnp.clip(array, -most, most).astype(dtype)


def setup_inputs(seed: int = 0) -> dict:
    seeds = jax.random.split(jax.random.key(seed), 8)
    return {
        "grad_out": normal_values(seeds[0], (SEQS, TOKENS, FF), 1.0, 6.0, ((0, 32), (2, 8))),
        "act_in": normal_values(seeds[1], (SEQS, TOKENS, D), 1.0, 6.0, ((0, 32), (2, 8))),
        "basis_out": normal_values(seeds[2], (FF, FF), FF ** -0.5, 0.046875, ((0, 8), (1, 32))),
        "basis_in": normal_values(seeds[3], (D, D), D ** -0.5, 0.09375, ((0, 8), (1, 32))),
        "eigen_vals": jnp.clip(jnp.exp(math.log(4.0) - 2.7725887 * jax.random.uniform(seeds[4], (FF, D), jnp.float32) ** block_scale(seeds[4], (FF, D), ((0, 32),), -0.2, 0.2)), 0.25, 4.0).astype(jnp.bfloat16),
        "query_out": normal_values(seeds[5], (QUERIES, RANK, FF), (FF * 16) ** -0.5, 0.01171875, ((2, 8),)),
        "query_in": normal_values(seeds[6], (QUERIES, RANK, D), (D * 64) ** -0.5, 0.01171875, ((2, 8),)),
    }


def rotate_blocks(data, basis, blocks):
    width = data.shape[1] // blocks
    data_blocks = data.reshape(data.shape[0], blocks, width).transpose(1, 0, 2)
    basis_blocks = basis.reshape(blocks, width, basis.shape[1])

    def add_block(total, operands):
        product = jnp.dot(operands[0], operands[1], preferred_element_type=jnp.float32)
        rounded = lax.optimization_barrier(product.astype(jnp.bfloat16))
        return total + rounded.astype(jnp.float32), None

    start_total = jnp.zeros((data.shape[0], basis.shape[1]), jnp.float32)
    total, _ = lax.scan(add_block, start_total, (data_blocks, basis_blocks))
    return total.astype(jnp.bfloat16)


def reference(grad_out, act_in, basis_out, basis_in, eigen_vals, query_out, query_in):
    grad_rot = rotate_blocks(grad_out.reshape(-1, FF), basis_out, N_FACTOR).reshape(SEQS, TOKENS, FF)
    act_rot = rotate_blocks(act_in.reshape(-1, D), basis_in, N_FACTOR).reshape(SEQS, TOKENS, D)
    query_rot = jnp.einsum("qrk,ki->qri", query_out.astype(jnp.float32), basis_out.astype(jnp.float32))
    value_rot = jnp.einsum("qrk,kj->qrj", query_in.astype(jnp.float32), basis_in.astype(jnp.float32)).astype(jnp.bfloat16)
    value_mat = value_rot.reshape(QUERIES * RANK, D)
    eigen_float = eigen_vals.astype(jnp.float32)

    def per_sequence(operands):
        contracted = lax.dot_general(operands[0], operands[1], (((0,), (0,)), ((), ())), preferred_element_type=jnp.float32)
        scaled = (contracted / eigen_float).astype(jnp.bfloat16)
        weighted = lax.dot_general(scaled, value_mat, (((1,), (1,)), ((), ())), preferred_element_type=jnp.float32)
        weighted = weighted.reshape(FF, QUERIES, RANK)
        return jnp.einsum("iqr,qri->q", weighted, query_rot)

    return lax.map(per_sequence, (grad_rot, act_rot))
```

```python
import jax
import jax.numpy as jnp
from jax import lax
from jax.sharding import Mesh, PartitionSpec as P

AXES = ("y", "zh", "c", "zl", "x")
SIZES = (4, 4, 2, 2, 4)
BF = jnp.bfloat16
F32 = jnp.float32


def shift(value, axis, by):
    n = SIZES[AXES.index(axis)]
    return lax.ppermute(value, axis, [(i, (i + by) % n) for i in range(n)])


def ring(value, axis):
    half = value.shape[-2] // 2
    minus = shift(value, axis, 1)
    plus = shift(value, axis, -1)
    far_a = shift(minus[..., :half, :], axis, 1)
    far_b = shift(plus[..., half:, :], axis, -1)
    return value, plus, jnp.concatenate([far_a, far_b], axis=-2), minus


def exchange(value, axes):
    return lax.all_to_all(value, axes, 0, 0, tiled=True)


def spread(value, axes, n):
    return exchange(jnp.broadcast_to(value[None], (n,) + value.shape), axes)


def dot(a, b):
    return jnp.dot(a, b, preferred_element_type=F32)


def shards(grad_out, act_in, basis_out, basis_in, eigen_vals, query_out, query_in):
    yi, zi, ci, li = (lax.axis_index(a) for a in ("y", "zh", "c", "zl"))
    tokens, unit = grad_out.shape[1:]
    queries, rank = query_out.shape[:2]
    rows = queries * rank
    half_rows = rows // 2
    width = basis_out.shape[1]
    first = ci == 0

    out_pair = (basis_out, shift(basis_out, "c", 1))
    in_other = shift(basis_in, "c", 1)
    in_both = jnp.where(
        first, jnp.concatenate([basis_in, in_other], 1), jnp.concatenate([in_other, basis_in], 1)
    )
    eigen = jnp.concatenate([eigen_vals, shift(eigen_vals, "c", 1)], 0)

    act = spread(act_in[0], "zh", 4)
    act = spread(act, "y", 4)
    part = dot(act.reshape(-1, act.shape[-1]), in_both).astype(BF)
    both = part.shape[-1]
    part = part.reshape(4, 2, 2, tokens, both).transpose(2, 0, 1, 3, 4)
    act_sum = exchange(part.reshape(8, 2, tokens, both), ("zl", "x")).reshape(8, 2, tokens, both)
    act_sum = act_sum.astype(F32).sum(0).astype(BF)
    act_rot = spread(spread(act_sum, "zh", 4), "y", 4).reshape(16, 2, tokens, both)

    mine = lax.dynamic_slice_in_dim(query_out.reshape(rows, unit), ci * half_rows, half_rows, 0)
    mine_in = lax.dynamic_slice_in_dim(
        query_in.reshape(rows, -1), ci * half_rows, half_rows, 0
    )
    query = jnp.concatenate(
        [dot(mine, out_pair[0]), dot(mine, out_pair[1]), dot(mine_in, in_both)], 1
    ).astype(BF)
    some = half_rows // 8
    query = exchange(query.reshape(8, some, -1), ("zl", "x")).reshape(8, some, -1)
    query = query.astype(F32).sum(0).astype(BF)
    value = spread(query[:, 2 * width :], ("y", "zh"), 16).reshape(16, some, both)
    value = value.transpose(1, 0, 2).reshape(some, 16 * both)
    query = spread(jnp.concatenate([query[:, : 2 * width], value], 1), ("zl", "x"), 8)
    query = query.reshape(half_rows, -1)
    swapped = jnp.concatenate(
        [query[:, width : 2 * width], query[:, :width], query[:, 2 * width :]], 1
    )
    query = jnp.concatenate([query, shift(swapped, "c", 1)], 0)
    query_rot = query[:, : 2 * width].astype(F32)
    value_rot = query[:, 2 * width :]

    blocks = []
    for block in ring(grad_out, "zh"):
        found = jnp.concatenate(ring(block, "y"), 0)
        flat = found.reshape(-1, unit)
        product = jnp.concatenate([dot(flat, out_pair[0]), dot(flat, out_pair[1])], 1).astype(BF)
        product = product.reshape(4, tokens, 2 * width)
        product = jnp.roll(product, yi, axis=0)
        product = exchange(product, "x").astype(F32).sum(0)
        blocks.append(product)
    same = li == zi % 2
    own, plus, far, minus = blocks
    slots = []
    for a, b in ((own, minus), (far, plus)):
        keep = jnp.where(same, a, b)
        give = jnp.where(same, b, a).astype(BF)
        slots.append((keep.astype(BF).astype(F32) + shift(give, "zl", 1).astype(F32)).astype(BF))
    low = jnp.where(same, zi, (zi + 3) % 4) // 2

    results = []
    for slot, grad in enumerate(slots):
        which = low if slot == 0 else 1 - low
        one = lax.dynamic_index_in_dim(act_rot, which, 1, False)
        one = one.transpose(1, 0, 2).reshape(tokens, -1)
        contracted = lax.dot_general(grad, one, (((0,), (0,)), ((), ())), preferred_element_type=F32)
        scaled = (contracted / eigen.astype(F32)).astype(BF)
        weighted = lax.dot_general(
            scaled, value_rot, (((1,), (1,)), ((), ())), preferred_element_type=F32
        )
        results.append((weighted * query_rot.T).sum(0))
    result = jnp.stack(results).reshape(2, queries, rank).sum(-1)
    result = jnp.where(low == 0, result, result[::-1])
    turned = jnp.concatenate([result[:, queries // 2 :], result[:, : queries // 2]], 1)
    result = jnp.where(first, result, turned)
    result = spread(result, ("y", "zh"), 16).reshape(16, 2, queries).sum(0)
    result = spread(result, ("c", "zl", "x"), 16).reshape(2, 2, 4, 2, queries)
    result = result.transpose(2, 3, 1, 0, 4).reshape(8, 4, queries)
    return lax.dynamic_index_in_dim(result, li * 4 + lax.axis_index("x"), 0, False)


def solution(mesh):
    fine = Mesh(mesh.devices.reshape(SIZES), AXES)
    dp, factor = ("y", "zh", "c"), ("zl", "x")
    in_specs = (
        P(dp, None, factor),
        P(dp, None, factor),
        P(factor, dp),
        P(factor, dp),
        P(dp, None),
        P(None, None, factor),
        P(None, None, factor),
    )
    return jax.shard_map(
        shards, mesh=fine, in_specs=in_specs, out_specs=P(factor, None), check_vma=False
    )
```

```python
import jax
import jax.numpy as jnp
from jax import lax
from jax.experimental import pallas as pl
from jax.experimental.pallas import tpu as pltpu
from jax.sharding import Mesh, PartitionSpec as P


AXES = ("y", "zh", "c", "zl", "x")
SIZES = (4, 4, 2, 2, 4)
BF = jnp.bfloat16
F32 = jnp.float32


def shift(value, axis, by):
    n = SIZES[AXES.index(axis)]
    return lax.ppermute(value, axis, [(i, (i + by) % n) for i in range(n)])


def gather(value, axis):
    return jnp.stack([value] + [shift(value, axis, -by) for by in (1, 2, 3)])


def exchange(value, axes):
    return lax.all_to_all(value, axes, 0, 0, tiled=True)


def spread(value, axes, n):
    return exchange(jnp.broadcast_to(value[None], (n,) + value.shape), axes)


def dot(a, b):
    return jnp.dot(a, b, preferred_element_type=F32)


def dot_t(a, b):
    return lax.dot_general(a, b, (((1,), (1,)), ((), ())), preferred_element_type=F32)


def rotate_in_kernel(at_ref, act, w, out):
    y = lax.rem(at_ref[0] + pl.program_id(0), 4)
    for z in range(4):
        zh = lax.rem(at_ref[1] + z, 4)
        out[lax.rem(zh, 2), y, zh // 2] = dot(act[0, z], w[...]).astype(BF)


def rotate_in(at, act, w):
    tokens, unit = act.shape[2:]
    n = w.shape[1]
    spec = pltpu.PrefetchScalarGridSpec(
        num_scalar_prefetch=1,
        grid=(4,),
        in_specs=[
            pl.BlockSpec((1, 4, tokens, unit), lambda y, _: (y, 0, 0, 0)),
            pl.BlockSpec((unit, n), lambda y, _: (0, 0)),
        ],
        out_specs=pl.BlockSpec((2, 4, 2, tokens, n), lambda y, _: (0, 0, 0, 0, 0)),
    )
    return pl.pallas_call(
        rotate_in_kernel,
        grid_spec=spec,
        out_shape=jax.ShapeDtypeStruct((2, 4, 2, tokens, n), BF),
        cost_estimate=pl.CostEstimate(
            flops=2 * 16 * tokens * unit * n, bytes_accessed=2 * 16 * tokens * (unit + n), transcendentals=0
        ),
        name="rotate_in",
    )(at, act, w)


def score_kernel(at_ref, grad, act, eig0, eig1, value, query, out, flipped, total):
    step = pl.program_id(0)
    n = eig0.shape[0]
    width = act.shape[4]

    @pl.when(step == 0)
    def _():
        for s in range(2):
            flipped[s] = grad[s].T
        total[...] = jnp.zeros_like(total)

    def body(e, _):
        zh = lax.rem(at_ref[1] + e, 4)
        cols = pl.ds(pl.multiple_of(zh * width, width), width)
        held = value[:, cols]
        for k, eig in enumerate((eig0, eig1)):
            here = slice(k * n, (k + 1) * n)
            inverse = 1.0 / eig[:, cols].astype(F32)
            for s in range(2):
                which = at_ref[2] if s == 0 else 1 - at_ref[2]
                contracted = dot(flipped[s, here, :], act[0, e, which])
                total[s, here, :] += dot_t((contracted * inverse).astype(BF), held)
        return 0

    lax.fori_loop(0, 4, body, 0)

    @pl.when(step == pl.num_programs(0) - 1)
    def _():
        for s in range(2):
            out[s : s + 1, :] = (total[s] * query[...]).sum(0, keepdims=True)


def score(at, grad, act, eig0, eig1, value, query):
    _, tokens, both = grad.shape
    n = eig0.shape[0]
    width = act.shape[4]
    cols = 4 * width
    rows = value.shape[0]
    spec = pltpu.PrefetchScalarGridSpec(
        num_scalar_prefetch=1,
        grid=(4,),
        in_specs=[
            pl.BlockSpec((2, tokens, both), lambda j, at: (0, 0, 0)),
            pl.BlockSpec((1, 4, 2, tokens, width), lambda j, at: (j, 0, 0, 0, 0)),
            pl.BlockSpec((n, cols), lambda j, at: (0, lax.rem(at[0] + j, 4))),
            pl.BlockSpec((n, cols), lambda j, at: (0, lax.rem(at[0] + j, 4))),
            pl.BlockSpec((rows, cols), lambda j, at: (0, lax.rem(at[0] + j, 4))),
            pl.BlockSpec((both, rows), lambda j, at: (0, 0)),
        ],
        out_specs=pl.BlockSpec((8, rows), lambda j, at: (0, 0)),
        scratch_shapes=[pltpu.VMEM((2, both, tokens), BF), pltpu.VMEM((2, both, rows), F32)],
    )
    return pl.pallas_call(
        score_kernel,
        grid_spec=spec,
        out_shape=jax.ShapeDtypeStruct((8, rows), F32),
        cost_estimate=pl.CostEstimate(
            flops=2 * 2 * both * 4 * cols * (tokens + rows),
            bytes_accessed=2 * both * 4 * cols,
            transcendentals=0,
        ),
        name="score",
    )(at, grad, act, eig0, eig1, value, query)


def shards(grad_out, act_in, basis_out, basis_in, eigen_vals, query_out, query_in):
    yi, zi, ci, li = (lax.axis_index(a) for a in ("y", "zh", "c", "zl"))
    tokens, unit = grad_out.shape[1:]
    queries, rank = query_out.shape[:2]
    rows = queries * rank
    half_rows = rows // 2
    width = basis_out.shape[1]
    first = ci == 0

    same = li == zi % 2
    low = jnp.where(same, zi, (zi + 3) % 4) // 2
    at = jnp.stack([yi, zi, low]).astype(jnp.int32)

    out_t = basis_out.T
    out_both = jnp.concatenate([out_t, shift(out_t, "c", 1)], 0)
    in_other = shift(basis_in, "c", 1)
    in_both = jnp.where(
        first, jnp.concatenate([basis_in, in_other], 1), jnp.concatenate([in_other, basis_in], 1)
    )
    eigen_other = shift(eigen_vals, "c", 1)

    act = gather(gather(act_in[0], "zh"), "y")
    part = rotate_in(at, act, in_both)
    both = part.shape[-1]
    act_sum = exchange(part.reshape(8, 2, tokens, both), ("zl", "x"))
    act_sum = act_sum.reshape(8, 2, tokens, both).astype(F32).sum(0).astype(BF)
    act_rot = gather(gather(act_sum, "zh"), "y")

    mine = lax.dynamic_slice_in_dim(query_out.reshape(rows, unit), ci * half_rows, half_rows, 0)
    mine_in = lax.dynamic_slice_in_dim(query_in.reshape(rows, -1), ci * half_rows, half_rows, 0)
    query = jnp.concatenate([dot_t(mine, out_both), dot(mine_in, in_both)], 1).astype(BF)
    some = half_rows // 8
    query = exchange(query.reshape(8, some, -1), ("zl", "x")).reshape(8, some, -1)
    query = query.astype(F32).sum(0).astype(BF)
    value = spread(query[:, 2 * width :], ("y", "zh"), 16).reshape(16, some, both)
    value = value.transpose(1, 0, 2).reshape(some, 16 * both)
    query = spread(jnp.concatenate([query[:, : 2 * width], value], 1), ("zl", "x"), 8)
    query = query.reshape(half_rows, -1)
    swapped = jnp.concatenate(
        [query[:, width : 2 * width], query[:, :width], query[:, 2 * width :]], 1
    )
    query = jnp.concatenate([query, shift(swapped, "c", 1)], 0)
    query_rot = query[:, : 2 * width].astype(F32).T
    value_rot = query[:, 2 * width :]

    grad = grad_out[0]
    plus, far, minus = (shift(grad, "zh", -by) for by in (1, 2, 3))
    blocks = []
    for some_blocks in ((grad,), (plus, minus), (far,)):
        some_blocks = jnp.stack(some_blocks)
        found = lax.all_gather(some_blocks, "y", axis=0, tiled=True)
        product = dot_t(found.reshape(-1, unit), out_both).astype(BF)
        product = exchange(product.reshape(-1, tokens, 2 * width), "x")
        product = product.reshape(4, -1, tokens, 2 * width).astype(F32).sum(0)
        blocks.extend(product[b] for b in range(product.shape[0]))
    own, plus, minus, far = blocks
    slots = []
    for k, (a, b) in enumerate(((own, minus), (plus, far))):
        mine_first = same if k == 0 else ~same
        keep = jnp.where(mine_first, a, b)
        give = jnp.where(mine_first, b, a).astype(BF)
        if k == 0:
            give, keep = lax.optimization_barrier((give, keep))
        got = shift(give, "zl", 1)
        slots.append((keep.astype(BF).astype(F32) + got.astype(F32)).astype(BF))

    result = score(at, jnp.stack(slots), act_rot, eigen_vals, eigen_other, value_rot, query_rot)[:2]
    result = result.reshape(2, queries, rank).sum(-1)
    result = jnp.where(low == 0, result, result[::-1])
    turned = jnp.concatenate([result[:, queries // 2 :], result[:, : queries // 2]], 1)
    result = jnp.where(first, result, turned)
    result = spread(result, ("y", "zh"), 16).reshape(16, 2, queries).sum(0)
    result = spread(result, ("c", "zl", "x"), 16).reshape(2, 2, 4, 2, queries)
    result = result.transpose(2, 3, 1, 0, 4).reshape(8, 4, queries)
    return lax.dynamic_index_in_dim(result, li * 4 + lax.axis_index("x"), 0, False)


def solution(mesh):
    fine = Mesh(mesh.devices.reshape(SIZES), AXES)
    dp, factor = ("y", "zh", "c"), ("zl", "x")
    in_specs = (
        P(dp, None, factor),
        P(dp, None, factor),
        P(factor, dp),
        P(factor, dp),
        P(dp, None),
        P(None, None, factor),
        P(None, None, factor),
    )

    return jax.shard_map(
        shards, mesh=fine, in_specs=in_specs, out_specs=P(factor, None), check_vma=False
    )
```

```python
import jax
import jax.numpy as jnp
from jax import lax
from jax.experimental import pallas as pl
from jax.experimental.pallas import tpu as pltpu
from jax.sharding import Mesh, PartitionSpec as P


AXES = ("y", "zh", "c", "zl", "x")
SIZES = (4, 4, 2, 2, 4)
BF = jnp.bfloat16
F32 = jnp.float32


def shift(value, axis, by):
    n = SIZES[AXES.index(axis)]
    return lax.ppermute(value, axis, [(i, (i + by) % n) for i in range(n)])


def gather(value, axis):
    return [value] + [shift(value, axis, -by) for by in (1, 2, 3)]


def from_owner(value, by):
    pairs = [(2 * h + h % 2, 2 * ((h - by) % 4) + h % 2) for h in range(4)]
    return lax.ppermute(value, ("zh", "zl"), pairs)


def to_owner(value):
    pairs = [(2 * h + 1 - h % 2, 2 * h + h % 2) for h in range(4)]
    return lax.ppermute(value, ("zh", "zl"), pairs)


def exchange(value, axes):
    return lax.all_to_all(value, axes, 0, 0, tiled=True)


def spread(value, axes, n):
    return exchange(jnp.broadcast_to(value[None], (n,) + value.shape), axes)


def dot(a, b):
    return jnp.dot(a, b, preferred_element_type=F32)


def dot_t(a, b):
    return lax.dot_general(a, b, (((1,), (1,)), ((), ())), preferred_element_type=F32)


def rotate_in_kernel(at_ref, a0, a1, a2, a3, w0, w1, w2, w3, out, act):
    tokens = a0.shape[0]
    n = w0.shape[1]
    for d, a in enumerate((a0, a1, a2, a3)):
        y = lax.rem(at_ref[0] + d, 4)
        act[pl.ds(pl.multiple_of(y * tokens, tokens), tokens), :] = a[...]
    for d, w in enumerate((w0, w1, w2, w3)):
        zh = lax.rem(at_ref[1] + d, 4)
        out[:, pl.ds(pl.multiple_of(zh * n, n), n)] = dot(act[...], w[...]).astype(BF)


def rotate_in(at, acts, bases):
    tokens, unit = acts[0].shape
    n = bases[0].shape[1]
    vmem = pl.BlockSpec(memory_space=pltpu.VMEM)
    return pl.pallas_call(
        rotate_in_kernel,
        in_specs=[pl.BlockSpec(memory_space=pltpu.SMEM)] + [vmem] * 8,
        out_specs=vmem,
        out_shape=jax.ShapeDtypeStruct((4 * tokens, 4 * n), BF),
        scratch_shapes=[pltpu.VMEM((4 * tokens, unit), BF)],
        cost_estimate=pl.CostEstimate(
            flops=2 * 16 * tokens * unit * n, bytes_accessed=2 * 16 * tokens * (unit + n), transcendentals=0
        ),
        name="rotate_in",
    )(at, *acts, *bases)


def score_kernel(at_ref, grad, act, eig0, eig1, value, query, out, flipped, total):
    step = pl.program_id(0)
    n = eig0.shape[0]
    width = act.shape[3] // 4

    @pl.when(step == 0)
    def _():
        for s in range(2):
            flipped[s] = grad[s].T
        total[...] = jnp.zeros_like(total)

    def body(e, _):
        cols = pl.ds(pl.multiple_of(e * width, width), width)
        held = value[:, cols]
        for k, eig in enumerate((eig0, eig1)):
            here = slice(k * n, (k + 1) * n)
            inverse = 1.0 / eig[:, cols].astype(F32)
            for s in range(2):
                contracted = dot(flipped[s, here, :], act[0, s, :, cols])
                total[s, here, :] += dot_t((contracted * inverse).astype(BF), held)
        return 0

    lax.fori_loop(0, 4, body, 0)

    @pl.when(step == pl.num_programs(0) - 1)
    def _():
        for s in range(2):
            out[s : s + 1, :] = (total[s] * query[...]).sum(0, keepdims=True)


def score(at, grad, act, eig0, eig1, value, query):
    _, tokens, both = grad.shape
    n = eig0.shape[0]
    cols = act.shape[3]
    rows = value.shape[0]
    spec = pltpu.PrefetchScalarGridSpec(
        num_scalar_prefetch=1,
        grid=(4,),
        in_specs=[
            pl.BlockSpec((2, tokens, both), lambda j, at: (0, 0, 0)),
            pl.BlockSpec((1, 2, tokens, cols), lambda j, at: (j, 0, 0, 0)),
            pl.BlockSpec((n, cols), lambda j, at: (0, lax.rem(at[0] + j, 4))),
            pl.BlockSpec((n, cols), lambda j, at: (0, lax.rem(at[0] + j, 4))),
            pl.BlockSpec((rows, cols), lambda j, at: (0, lax.rem(at[0] + j, 4))),
            pl.BlockSpec((both, rows), lambda j, at: (0, 0)),
        ],
        out_specs=pl.BlockSpec((8, rows), lambda j, at: (0, 0)),
        scratch_shapes=[pltpu.VMEM((2, both, tokens), BF), pltpu.VMEM((2, both, rows), F32)],
    )
    return pl.pallas_call(
        score_kernel,
        grid_spec=spec,
        out_shape=jax.ShapeDtypeStruct((8, rows), F32),
        cost_estimate=pl.CostEstimate(
            flops=2 * 2 * both * 4 * cols * (tokens + rows),
            bytes_accessed=2 * both * 4 * cols,
            transcendentals=0,
        ),
        name="score",
    )(at, grad, act, eig0, eig1, value, query)


def shards(grad_out, act_in, basis_out, basis_in, eigen_vals, query_out, query_in):
    yi, zi, ci, li = (lax.axis_index(a) for a in ("y", "zh", "c", "zl"))
    tokens, unit = grad_out.shape[1:]
    queries, rank = query_out.shape[:2]
    rows = queries * rank
    half_rows = rows // 2
    width = basis_out.shape[1]
    first = ci == 0

    same = li == zi % 2
    low = jnp.where(same, zi, (zi + 3) % 4) // 2
    at = jnp.stack([yi, zi]).astype(jnp.int32)

    out_t = basis_out.T
    out_both = jnp.concatenate([out_t, shift(out_t, "c", 1)], 0)
    out_both = lax.optimization_barrier(out_both)
    in_other = shift(basis_in, "c", 1)
    in_both = jnp.where(
        first, jnp.concatenate([basis_in, in_other], 1), jnp.concatenate([in_other, basis_in], 1)
    )
    both = in_both.shape[1]
    eigen_other = shift(eigen_vals, "c", 1)

    part = rotate_in(at, gather(act_in[0], "y"), gather(in_both, "zh"))
    part = exchange(part.reshape(4, tokens, 4 * both), "x").astype(F32).sum(0).astype(BF)
    part = (part.astype(F32) + to_owner(part).astype(F32)).astype(BF)
    plus, far, minus = (from_owner(part, by) for by in (1, 2, 3))
    act_rot = jnp.stack([jnp.where(same, part, minus), jnp.where(same, far, plus)])
    act_rot = jnp.stack(gather(act_rot, "y"))

    mine = lax.dynamic_slice_in_dim(query_out.reshape(rows, unit), ci * half_rows, half_rows, 0)
    mine_in = lax.dynamic_slice_in_dim(query_in.reshape(rows, -1), ci * half_rows, half_rows, 0)
    query = jnp.concatenate([dot_t(mine, out_both), dot(mine_in, in_both)], 1).astype(BF)
    some = half_rows // 8
    query = exchange(query.reshape(8, some, -1), ("zl", "x")).reshape(8, some, -1)
    query = query.astype(F32).sum(0).astype(BF)
    value = spread(query[:, 2 * width :], ("y", "zh"), 16).reshape(16, some, both)
    value = value.transpose(1, 0, 2).reshape(some, 16 * both)
    query = spread(jnp.concatenate([query[:, : 2 * width], value], 1), ("zl", "x"), 8)
    query = query.reshape(half_rows, -1)
    swapped = jnp.concatenate(
        [query[:, width : 2 * width], query[:, :width], query[:, 2 * width :]], 1
    )
    query = jnp.concatenate([query, shift(swapped, "c", 1)], 0)
    query_rot = query[:, : 2 * width].astype(F32).T
    value_rot = query[:, 2 * width :]

    grad = grad_out[0]
    plus, far, minus = (shift(grad, "zh", -by) for by in (1, 2, 3))
    blocks = []
    for some_blocks in ((grad,), (plus, minus), (far,)):
        some_blocks = jnp.stack(some_blocks)
        found = lax.all_gather(some_blocks, "y", axis=0, tiled=True)
        product = dot_t(found.reshape(-1, unit), out_both).astype(BF)
        product = exchange(product.reshape(-1, tokens, 2 * width), "x")
        product = product.reshape(4, -1, tokens, 2 * width).astype(F32).sum(0)
        blocks.extend(product[b] for b in range(product.shape[0]))
    own, plus, minus, far = blocks
    keep = jnp.stack([jnp.where(same, own, minus), jnp.where(same, far, plus)])
    give = jnp.stack([jnp.where(same, minus, own), jnp.where(same, plus, far)])
    got = shift(give.astype(BF), "zl", 1)
    slots = (keep.astype(BF).astype(F32) + got.astype(F32)).astype(BF)

    result = score(at, slots, act_rot, eigen_vals, eigen_other, value_rot, query_rot)[:2]
    result = result.reshape(2, queries, rank).sum(-1)
    result = jnp.where(low == 0, result, result[::-1])
    turned = jnp.concatenate([result[:, queries // 2 :], result[:, : queries // 2]], 1)
    result = jnp.where(first, result, turned)
    result = spread(result, ("y", "zh"), 16).reshape(16, 2, queries).sum(0)
    result = spread(result, ("c", "zl", "x"), 16).reshape(2, 2, 4, 2, queries)
    result = result.transpose(2, 3, 1, 0, 4).reshape(8, 4, queries)
    return lax.dynamic_index_in_dim(result, li * 4 + lax.axis_index("x"), 0, False)


def solution(mesh):
    fine = Mesh(mesh.devices.reshape(SIZES), AXES)
    dp, factor = ("y", "zh", "c"), ("zl", "x")
    in_specs = (
        P(dp, None, factor),
        P(dp, None, factor),
        P(factor, dp),
        P(factor, dp),
        P(dp, None),
        P(None, None, factor),
        P(None, None, factor),
    )

    return jax.shard_map(
        shards, mesh=fine, in_specs=in_specs, out_specs=P(factor, None), check_vma=False
    )
```

```python
import jax
import jax.numpy as jnp
from jax import lax
from jax.experimental import pallas as pl
from jax.experimental.pallas import tpu as pltpu
from jax.sharding import Mesh, PartitionSpec as P


AXES = ("y", "zh", "c", "zl", "x")
SIZES = (4, 4, 2, 2, 4)
BF = jnp.bfloat16
F32 = jnp.float32


def shift(value, axis, by):
    n = SIZES[AXES.index(axis)]
    return lax.ppermute(value, axis, [(i, (i + by) % n) for i in range(n)])


def gather(value, axis):
    return [value] + [shift(value, axis, -by) for by in (1, 2, 3)]


def from_owner(value, by):
    pairs = [(2 * h + h % 2, 2 * ((h - by) % 4) + h % 2) for h in range(4)]
    return lax.ppermute(value, ("zh", "zl"), pairs)


def to_owner(value):
    pairs = [(2 * h + 1 - h % 2, 2 * h + h % 2) for h in range(4)]
    return lax.ppermute(value, ("zh", "zl"), pairs)


def exchange(value, axes):
    return lax.all_to_all(value, axes, 0, 0, tiled=True)


def spread(value, axes, n):
    return exchange(jnp.broadcast_to(value[None], (n,) + value.shape), axes)


def dot(a, b):
    return jnp.dot(a, b, preferred_element_type=F32)


def dot_t(a, b):
    return lax.dot_general(a, b, (((1,), (1,)), ((), ())), preferred_element_type=F32)


def rotate_in_kernel(at_ref, a0, a1, a2, a3, w0, w1, out, act):
    tokens = a0.shape[0]
    n = w0.shape[2]
    for d, a in enumerate((a0, a1, a2, a3)):
        y = lax.rem(at_ref[0] + d, 4)
        act[pl.ds(pl.multiple_of(y * tokens, tokens), tokens), :] = a[...]
    for k, w in enumerate((w0, w1)):
        core = at_ref[2] if k == 0 else 1 - at_ref[2]
        for d in range(4):
            zh = lax.rem(at_ref[1] + d, 4)
            here = pl.multiple_of((2 * zh + core) * n, n)
            out[:, pl.ds(here, n)] = dot(act[...], w[d]).astype(BF)


def rotate_in(at, acts, bases):
    tokens, unit = acts[0].shape
    n = bases[0].shape[2]
    vmem = pl.BlockSpec(memory_space=pltpu.VMEM)
    return pl.pallas_call(
        rotate_in_kernel,
        in_specs=[pl.BlockSpec(memory_space=pltpu.SMEM)] + [vmem] * 6,
        out_specs=vmem,
        out_shape=jax.ShapeDtypeStruct((4 * tokens, 8 * n), BF),
        scratch_shapes=[pltpu.VMEM((4 * tokens, unit), BF)],
        cost_estimate=pl.CostEstimate(
            flops=2 * 32 * tokens * unit * n, bytes_accessed=2 * 16 * tokens * (unit + n), transcendentals=0
        ),
        name="rotate_in",
    )(at, *acts, *bases)


def score_kernel(at_ref, grad, act, eig0, eig1, value, query, out, flipped, total):
    step = pl.program_id(0)
    n = eig0.shape[0]
    width = act.shape[3] // 4

    @pl.when(step == 0)
    def _():
        for s in range(2):
            flipped[s] = grad[s].T
        total[...] = jnp.zeros_like(total)

    def body(e, _):
        cols = pl.ds(pl.multiple_of(e * width, width), width)
        held = value[:, cols]
        for k, eig in enumerate((eig0, eig1)):
            here = slice(k * n, (k + 1) * n)
            inverse = 1.0 / eig[:, cols].astype(F32)
            for s in range(2):
                contracted = dot(flipped[s, here, :], act[0, s, :, cols])
                total[s, here, :] += dot_t((contracted * inverse).astype(BF), held)
        return 0

    lax.fori_loop(0, 4, body, 0)

    @pl.when(step == pl.num_programs(0) - 1)
    def _():
        for s in range(2):
            out[s : s + 1, :] = (total[s] * query[...]).sum(0, keepdims=True)


def score(at, grad, act, eig0, eig1, value, query):
    _, tokens, both = grad.shape
    n = eig0.shape[0]
    cols = act.shape[3]
    rows = value.shape[0]
    spec = pltpu.PrefetchScalarGridSpec(
        num_scalar_prefetch=1,
        grid=(4,),
        in_specs=[
            pl.BlockSpec((2, tokens, both), lambda j, at: (0, 0, 0)),
            pl.BlockSpec((1, 2, tokens, cols), lambda j, at: (j, 0, 0, 0)),
            pl.BlockSpec((n, cols), lambda j, at: (0, lax.rem(at[0] + j, 4))),
            pl.BlockSpec((n, cols), lambda j, at: (0, lax.rem(at[0] + j, 4))),
            pl.BlockSpec((rows, cols), lambda j, at: (0, lax.rem(at[0] + j, 4))),
            pl.BlockSpec((both, rows), lambda j, at: (0, 0)),
        ],
        out_specs=pl.BlockSpec((8, rows), lambda j, at: (0, 0)),
        scratch_shapes=[pltpu.VMEM((2, both, tokens), BF), pltpu.VMEM((2, both, rows), F32)],
    )
    return pl.pallas_call(
        score_kernel,
        grid_spec=spec,
        out_shape=jax.ShapeDtypeStruct((8, rows), F32),
        cost_estimate=pl.CostEstimate(
            flops=2 * 2 * both * 4 * cols * (tokens + rows),
            bytes_accessed=2 * both * 4 * cols,
            transcendentals=0,
        ),
        name="score",
    )(at, grad, act, eig0, eig1, value, query)


def shards(grad_out, act_in, basis_out, basis_in, eigen_vals, query_out, query_in):
    yi, zi, ci, li = (lax.axis_index(a) for a in ("y", "zh", "c", "zl"))
    tokens, unit = grad_out.shape[1:]
    queries, rank = query_out.shape[:2]
    rows = queries * rank
    half_rows = rows // 2
    width = basis_out.shape[1]
    first = ci == 0

    same = li == zi % 2
    low = jnp.where(same, zi, (zi + 3) % 4) // 2
    at = jnp.stack([yi, zi, ci]).astype(jnp.int32)

    out_t = basis_out.T
    out_both = jnp.concatenate([out_t, shift(out_t, "c", 1)], 0)
    out_both = lax.optimization_barrier(out_both)
    eigen_other = shift(eigen_vals, "c", 1)

    in_own = jnp.stack(gather(basis_in, "zh"))
    in_other = shift(in_own, "c", 1)
    both = 2 * basis_in.shape[1]
    part = rotate_in(at, gather(act_in[0], "y"), (in_own, in_other))
    part = exchange(part.reshape(4, tokens, 4 * both), "x").astype(F32).sum(0).astype(BF)
    part = (part.astype(F32) + to_owner(part).astype(F32)).astype(BF)
    plus, far, minus = (from_owner(part, by) for by in (1, 2, 3))
    act_rot = jnp.stack([jnp.where(same, part, minus), jnp.where(same, far, plus)])
    act_rot = jnp.stack(gather(act_rot, "y"))

    mine = lax.dynamic_slice_in_dim(query_out.reshape(rows, unit), ci * half_rows, half_rows, 0)
    mine_in = lax.dynamic_slice_in_dim(query_in.reshape(rows, -1), ci * half_rows, half_rows, 0)
    in_both = jnp.concatenate(
        [jnp.where(first, basis_in, in_other[0]), jnp.where(first, in_other[0], basis_in)], 1
    )
    query = jnp.concatenate([dot_t(mine, out_both), dot(mine_in, in_both)], 1).astype(BF)
    some = half_rows // 8
    query = exchange(query.reshape(8, some, -1), ("zl", "x")).reshape(8, some, -1)
    query = query.astype(F32).sum(0).astype(BF)
    value = spread(query[:, 2 * width :], ("y", "zh"), 16).reshape(16, some, both)
    value = value.transpose(1, 0, 2).reshape(some, 16 * both)
    query = spread(jnp.concatenate([query[:, : 2 * width], value], 1), ("zl", "x"), 8)
    query = query.reshape(half_rows, -1)
    swapped = jnp.concatenate(
        [query[:, width : 2 * width], query[:, :width], query[:, 2 * width :]], 1
    )
    query = jnp.concatenate([query, shift(swapped, "c", 1)], 0)
    query_rot = query[:, : 2 * width].astype(F32).T
    value_rot = query[:, 2 * width :]

    grad = grad_out[0]
    plus, far, minus = (shift(grad, "zh", -by) for by in (1, 2, 3))
    blocks = []
    for some_blocks in ((grad,), (plus, minus), (far,)):
        some_blocks = jnp.stack(some_blocks)
        found = lax.all_gather(some_blocks, "y", axis=0, tiled=True)
        product = dot_t(found.reshape(-1, unit), out_both).astype(BF)
        product = exchange(product.reshape(-1, tokens, 2 * width), "x")
        product = product.reshape(4, -1, tokens, 2 * width).astype(F32).sum(0)
        blocks.extend(product[b] for b in range(product.shape[0]))
    own, plus, minus, far = blocks
    keep = jnp.stack([jnp.where(same, own, minus), jnp.where(same, far, plus)])
    give = jnp.stack([jnp.where(same, minus, own), jnp.where(same, plus, far)])
    got = shift(give.astype(BF), "zl", 1)
    slots = (keep.astype(BF).astype(F32) + got.astype(F32)).astype(BF)

    result = score(at, slots, act_rot, eigen_vals, eigen_other, value_rot, query_rot)[:2]
    result = result.reshape(2, queries, rank).sum(-1)
    result = jnp.where(low == 0, result, result[::-1])
    turned = jnp.concatenate([result[:, queries // 2 :], result[:, : queries // 2]], 1)
    result = jnp.where(first, result, turned)
    result = spread(result, ("y", "zh"), 16).reshape(16, 2, queries).sum(0)
    result = spread(result, ("c", "zl", "x"), 16).reshape(2, 2, 4, 2, queries)
    result = result.transpose(2, 3, 1, 0, 4).reshape(8, 4, queries)
    return lax.dynamic_index_in_dim(result, li * 4 + lax.axis_index("x"), 0, False)


def solution(mesh):
    fine = Mesh(mesh.devices.reshape(SIZES), AXES)
    dp, factor = ("y", "zh", "c"), ("zl", "x")
    in_specs = (
        P(dp, None, factor),
        P(dp, None, factor),
        P(factor, dp),
        P(factor, dp),
        P(dp, None),
        P(None, None, factor),
        P(None, None, factor),
    )

    return jax.shard_map(
        shards, mesh=fine, in_specs=in_specs, out_specs=P(factor, None), check_vma=False
    )
```

```python
import functools

import jax
import jax.numpy as jnp
from jax import lax
from jax.experimental import pallas as pl
from jax.experimental.pallas import tpu as pltpu
from jax.sharding import Mesh, PartitionSpec as P


AXES = ("y", "zh", "c", "zl", "x")
SIZES = (4, 4, 2, 2, 4)
BF = jnp.bfloat16
F32 = jnp.float32


def shift(value, axis, by):
    n = SIZES[AXES.index(axis)]
    return lax.ppermute(value, axis, [(i, (i + by) % n) for i in range(n)])


def gather(value, axis):
    return [value] + [shift(value, axis, -by) for by in (1, 2, 3)]


def from_owner(value, by):
    pairs = [(2 * h + h % 2, 2 * ((h - by) % 4) + h % 2) for h in range(4)]
    return lax.ppermute(value, ("zh", "zl"), pairs)


def to_owner(value):
    pairs = [(2 * h + 1 - h % 2, 2 * h + h % 2) for h in range(4)]
    return lax.ppermute(value, ("zh", "zl"), pairs)


def exchange(value, axes):
    return lax.all_to_all(value, axes, 0, 0, tiled=True)


def spread(value, axes, n):
    return exchange(jnp.broadcast_to(value[None], (n,) + value.shape), axes)


def dot(a, b):
    return jnp.dot(a, b, preferred_element_type=F32)


def dot_t(a, b):
    return lax.dot_general(a, b, (((1,), (1,)), ((), ())), preferred_element_type=F32)


def rotate_in_kernel(at_ref, a0, a1, a2, a3, q, w0, w1, out, value, act):
    tokens = a0.shape[0]
    n = w0.shape[2]
    for d, a in enumerate((a0, a1, a2, a3)):
        y = lax.rem(at_ref[0] + d, 4)
        act[pl.ds(pl.multiple_of(y * tokens, tokens), tokens), :] = a[...]
    act[4 * tokens :, :] = q[...]
    for k, w in enumerate((w0, w1)):
        core = at_ref[2] if k == 0 else 1 - at_ref[2]
        for d in range(4):
            zh = lax.rem(at_ref[1] + d, 4)
            here = pl.ds(pl.multiple_of((2 * zh + core) * n, n), n)
            product = dot(act[...], w[d]).astype(BF)
            out[:, here] = product[: 4 * tokens]
            value[:, here] = product[4 * tokens :]


def rotate_in(at, acts, query, bases):
    tokens, unit = acts[0].shape
    rows = query.shape[0]
    n = bases[0].shape[2]
    vmem = pl.BlockSpec(memory_space=pltpu.VMEM)
    return pl.pallas_call(
        rotate_in_kernel,
        in_specs=[pl.BlockSpec(memory_space=pltpu.SMEM)] + [vmem] * 7,
        out_specs=(vmem, vmem),
        out_shape=(
            jax.ShapeDtypeStruct((4 * tokens, 8 * n), BF),
            jax.ShapeDtypeStruct((rows, 8 * n), BF),
        ),
        scratch_shapes=[pltpu.VMEM((4 * tokens + rows, unit), BF)],
        cost_estimate=pl.CostEstimate(
            flops=2 * 32 * tokens * unit * n, bytes_accessed=2 * 16 * tokens * (unit + n), transcendentals=0
        ),
        name="rotate_in",
    )(at, *acts, query, *bases)


def split_kernel(flag, a, b, keep, give):
    def total(ref):
        return sum(ref[k, 0].astype(F32) for k in range(4)).astype(BF)

    @pl.when(flag[0] == 1)
    def _():
        keep[...] = total(a)
        give[...] = total(b)

    @pl.when(flag[0] == 0)
    def _():
        keep[...] = total(b)
        give[...] = total(a)


def split(flag, a, b):
    (left, at_left), (right, at_right) = a, b
    tokens, both = left.shape[2:]
    tile = tokens // 4
    block = (4, 1, tile, both)
    out = pl.BlockSpec((tile, both), lambda t, _: (t, 0))
    shape = jax.ShapeDtypeStruct((tokens, both), BF)
    spec = pltpu.PrefetchScalarGridSpec(
        num_scalar_prefetch=1,
        grid=(4,),
        in_specs=[
            pl.BlockSpec(block, lambda t, _: (0, at_left, t, 0)),
            pl.BlockSpec(block, lambda t, _: (0, at_right, t, 0)),
        ],
        out_specs=(out, out),
    )
    return pl.pallas_call(
        split_kernel,
        grid_spec=spec,
        out_shape=(shape, shape),
        cost_estimate=pl.CostEstimate(
            flops=8 * tokens * both, bytes_accessed=20 * tokens * both, transcendentals=0
        ),
        name="split",
    )(flag, left, right)


def score_kernel(slot, at_ref, keep, got, v0, v1, v2, v3, other, eig0, eig1, query, out, flipped, total, act, held):
    step = pl.program_id(0)
    n = eig0.shape[0]
    tokens = keep.shape[0]
    half = other.shape[1]
    width = act.shape[1] // 4

    @pl.when(step == 0)
    def _():
        grad = keep[...].astype(F32) + got[...].astype(F32)
        flipped[...] = grad.T.astype(BF)
        total[...] = jnp.zeros_like(total)

    for d, ref in enumerate((v0, v1, v2, v3)):

        @pl.when(step == d)
        def _(ref=ref):
            act[...] = ref[slot * tokens : (slot + 1) * tokens, :]
            held[:half, :] = ref[2 * tokens :, :]

    held[half:, :] = other[0]

    def body(e, _):
        cols = pl.ds(pl.multiple_of(e * width, width), width)
        for k, eig in enumerate((eig0, eig1)):
            here = slice(k * n, (k + 1) * n)
            contracted = dot(flipped[here, :], act[:, cols])
            scaled = (contracted * (1.0 / eig[:, cols].astype(F32))).astype(BF)
            total[here, :] += dot_t(scaled, held[:, cols])
        return 0

    lax.fori_loop(0, 4, body, 0)

    @pl.when(step == pl.num_programs(0) - 1)
    def _():
        out[0:1, :] = (total[...] * query[...]).sum(0, keepdims=True)


def score(slot, at, keep, got, acts, other, eig0, eig1, query):
    tokens, both = keep.shape
    n = eig0.shape[0]
    cols = acts[0].shape[1]
    half = other.shape[1]
    rows = 2 * half

    def whole(a):
        return pl.BlockSpec(a.shape, lambda j, at: (0,) * a.ndim)

    spec = pltpu.PrefetchScalarGridSpec(
        num_scalar_prefetch=1,
        grid=(4,),
        in_specs=[whole(keep), whole(got)]
        + [whole(a) for a in acts]
        + [
            pl.BlockSpec((1, half, cols), lambda j, at: (j, 0, 0)),
            pl.BlockSpec((n, cols), lambda j, at: (0, lax.rem(at[0] + j, 4))),
            pl.BlockSpec((n, cols), lambda j, at: (0, lax.rem(at[0] + j, 4))),
            whole(query),
        ],
        out_specs=pl.BlockSpec((8, rows), lambda j, at: (0, 0)),
        scratch_shapes=[
            pltpu.VMEM((both, tokens), BF),
            pltpu.VMEM((both, rows), F32),
            pltpu.VMEM((tokens, cols), BF),
            pltpu.VMEM((rows, cols), BF),
        ],
    )
    return pl.pallas_call(
        functools.partial(score_kernel, slot),
        grid_spec=spec,
        out_shape=jax.ShapeDtypeStruct((8, rows), F32),
        cost_estimate=pl.CostEstimate(
            flops=2 * both * 4 * cols * (tokens + rows),
            bytes_accessed=2 * both * 4 * cols,
            transcendentals=0,
        ),
    )(at, keep, got, *acts, other, eig0, eig1, query)[0]


def shards(grad_out, act_in, basis_out, basis_in, eigen_vals, query_out, query_in):
    yi, zi, ci, li = (lax.axis_index(a) for a in ("y", "zh", "c", "zl"))
    tokens, unit = grad_out.shape[1:]
    queries, rank = query_out.shape[:2]
    rows = queries * rank
    half_rows = rows // 2
    width = basis_out.shape[1]
    first = ci == 0

    same = li == zi % 2
    at = jnp.stack([yi, zi, ci]).astype(jnp.int32)

    out_t = basis_out.T
    out_both = jnp.concatenate([out_t, shift(out_t, "c", 1)], 0)
    out_both = lax.optimization_barrier(out_both)
    eigen_other = shift(eigen_vals, "c", 1)

    mine = lax.dynamic_slice_in_dim(query_out.reshape(rows, unit), ci * half_rows, half_rows, 0)
    mine_in = lax.dynamic_slice_in_dim(query_in.reshape(rows, -1), ci * half_rows, half_rows, 0)
    in_own = jnp.stack(gather(basis_in, "zh"))
    in_other = shift(in_own, "c", 1)
    part, value = rotate_in(at, gather(act_in[0], "y"), mine_in, (in_own, in_other))
    part = exchange(part.reshape(4, tokens, -1), "x").astype(F32).sum(0).astype(BF)
    part = (part.astype(F32) + to_owner(part).astype(F32)).astype(BF)
    plus, far, minus = (from_owner(part, by) for by in (1, 2, 3))

    query = jnp.concatenate([dot_t(mine, out_both).astype(BF), value], 1)
    some = half_rows // 8
    query = exchange(query.reshape(8, some, -1), ("zl", "x")).reshape(8, some, -1)
    query = query.astype(F32).sum(0).astype(BF)
    query = spread(query, ("zl", "x"), 8).reshape(half_rows, -1)
    value = query[:, 2 * width :]
    query = query[:, : 2 * width]
    swapped = jnp.concatenate([query[:, width:], query[:, :width]], 1)
    query = jnp.concatenate([query, shift(swapped, "c", 1)], 0)
    query_rot = query.astype(F32).T

    act_rot = jnp.concatenate(
        [jnp.where(same, part, minus), jnp.where(same, far, plus), value], 0
    )
    act_rot = gather(act_rot, "y")
    value_other = shift(jnp.stack([a[2 * tokens :] for a in act_rot]), "c", 1)

    grad = grad_out[0]
    plus, far, minus = (shift(grad, "zh", -by) for by in (1, 2, 3))
    blocks = []
    for some_blocks in ((grad,), (plus, minus), (far,)):
        some_blocks = jnp.stack(some_blocks)
        found = lax.all_gather(some_blocks, "y", axis=0, tiled=True)
        product = dot_t(found.reshape(-1, unit), out_both).astype(BF)
        product = exchange(product.reshape(-1, tokens, 2 * width), "x")
        blocks.append(product.reshape(4, -1, tokens, 2 * width))
    flag = same.astype(jnp.int32)[None]
    result = []
    for slot, (a, b, keeps) in enumerate(
        (((blocks[0], 0), (blocks[1], 1), flag), ((blocks[2], 0), (blocks[1], 0), flag))
    ):
        keep, give = split(keeps, a, b)
        got = shift(give, "zl", 1)
        result.append(
            score(slot, at, keep, got, act_rot, value_other, eigen_vals, eigen_other, query_rot)
        )
    result = jnp.stack(result)
    low = jnp.where(same, zi, (zi + 3) % 4) // 2

    result = result.reshape(2, queries, rank).sum(-1)
    result = jnp.where(low == 0, result, result[::-1])
    turned = jnp.concatenate([result[:, queries // 2 :], result[:, : queries // 2]], 1)
    result = jnp.where(first, result, turned)
    result = spread(result, ("y", "zh"), 16).reshape(16, 2, queries).sum(0)
    result = spread(result, ("c", "zl", "x"), 16).reshape(2, 2, 4, 2, queries)
    result = result.transpose(2, 3, 1, 0, 4).reshape(8, 4, queries)
    return lax.dynamic_index_in_dim(result, li * 4 + lax.axis_index("x"), 0, False)


def solution(mesh):
    fine = Mesh(mesh.devices.reshape(SIZES), AXES)
    dp, factor = ("y", "zh", "c"), ("zl", "x")
    in_specs = (
        P(dp, None, factor),
        P(dp, None, factor),
        P(factor, dp),
        P(factor, dp),
        P(dp, None),
        P(None, None, factor),
        P(None, None, factor),
    )

    return jax.shard_map(
        shards, mesh=fine, in_specs=in_specs, out_specs=P(factor, None), check_vma=False
    )
```

```python
import functools

import jax
import jax.numpy as jnp
from jax import lax
from jax.experimental import pallas as pl
from jax.experimental.pallas import tpu as pltpu
from jax.sharding import Mesh, PartitionSpec as P


AXES = ("y", "zh", "c", "zl", "x")
SIZES = (4, 4, 2, 2, 4)
BF = jnp.bfloat16
F32 = jnp.float32


def shift(value, axis, by):
    n = SIZES[AXES.index(axis)]
    return lax.ppermute(value, axis, [(i, (i + by) % n) for i in range(n)])


def gather(value, axis):
    return [value] + [shift(value, axis, -by) for by in (1, 2, 3)]


def from_owner(value, by):
    pairs = [(2 * h + h % 2, 2 * ((h - by) % 4) + h % 2) for h in range(4)]
    return lax.ppermute(value, ("zh", "zl"), pairs)


def to_owner(value):
    pairs = [(2 * h + 1 - h % 2, 2 * h + h % 2) for h in range(4)]
    return lax.ppermute(value, ("zh", "zl"), pairs)


def exchange(value, axes):
    return lax.all_to_all(value, axes, 0, 0, tiled=True)


def spread(value, axes, n):
    return exchange(jnp.broadcast_to(value[None], (n,) + value.shape), axes)


def dot(a, b):
    return jnp.dot(a, b, preferred_element_type=F32)


def dot_t(a, b):
    return lax.dot_general(a, b, (((1,), (1,)), ((), ())), preferred_element_type=F32)


def rotate_in_kernel(at_ref, a0, a1, a2, a3, q, w0, w1, out, value, act):
    tokens = a0.shape[0]
    n = w0.shape[2]
    for d, a in enumerate((a0, a1, a2, a3)):
        y = lax.rem(at_ref[0] + d, 4)
        act[pl.ds(pl.multiple_of(y * tokens, tokens), tokens), :] = a[...]
    act[4 * tokens :, :] = q[...]
    for k, w in enumerate((w0, w1)):
        core = at_ref[2] if k == 0 else 1 - at_ref[2]
        for d in range(4):
            zh = lax.rem(at_ref[1] + d, 4)
            here = pl.ds(pl.multiple_of((2 * zh + core) * n, n), n)
            product = dot(act[...], w[d]).astype(BF)
            out[:, here] = product[: 4 * tokens]
            value[:, here] = product[4 * tokens :]


def rotate_in(at, acts, query, bases):
    tokens, unit = acts[0].shape
    rows = query.shape[0]
    n = bases[0].shape[2]
    vmem = pl.BlockSpec(memory_space=pltpu.VMEM)
    return pl.pallas_call(
        rotate_in_kernel,
        in_specs=[pl.BlockSpec(memory_space=pltpu.SMEM)] + [vmem] * 7,
        out_specs=(vmem, vmem),
        out_shape=(
            jax.ShapeDtypeStruct((4 * tokens, 8 * n), BF),
            jax.ShapeDtypeStruct((rows, 8 * n), BF),
        ),
        scratch_shapes=[pltpu.VMEM((4 * tokens + rows, unit), BF)],
        cost_estimate=pl.CostEstimate(
            flops=2 * 32 * tokens * unit * n, bytes_accessed=2 * 16 * tokens * (unit + n), transcendentals=0
        ),
        name="rotate_in",
    )(at, *acts, query, *bases)


def split_kernel(flag, a, b, keep, give):
    def total(ref):
        return sum(ref[k, 0].astype(F32) for k in range(4)).astype(BF)

    @pl.when(flag[0] == 1)
    def _():
        keep[...] = total(a)
        give[...] = total(b)

    @pl.when(flag[0] == 0)
    def _():
        keep[...] = total(b)
        give[...] = total(a)


def split(flag, a, b):
    (left, at_left), (right, at_right) = a, b
    tokens, both = left.shape[2:]
    tile = tokens // 2
    block = (4, 1, tile, both)
    out = pl.BlockSpec((tile, both), lambda t, _: (t, 0))
    shape = jax.ShapeDtypeStruct((tokens, both), BF)
    spec = pltpu.PrefetchScalarGridSpec(
        num_scalar_prefetch=1,
        grid=(2,),
        in_specs=[
            pl.BlockSpec(block, lambda t, _: (0, at_left, t, 0)),
            pl.BlockSpec(block, lambda t, _: (0, at_right, t, 0)),
        ],
        out_specs=(out, out),
    )
    return pl.pallas_call(
        split_kernel,
        grid_spec=spec,
        out_shape=(shape, shape),
        cost_estimate=pl.CostEstimate(
            flops=8 * tokens * both, bytes_accessed=20 * tokens * both, transcendentals=0
        ),
        name="split",
    )(flag, left, right)


def score_kernel(slot, at_ref, keep, got, v0, v1, v2, v3, other, inv0, inv1, query, out, flipped, total, act, held):
    step = pl.program_id(0)
    n = inv0.shape[0]
    tokens = keep.shape[0]
    half = other.shape[1]
    width = act.shape[1] // 4

    @pl.when(step == 0)
    def _():
        grad = keep[...].astype(F32) + got[...].astype(F32)
        flipped[...] = grad.T.astype(BF)
        total[...] = jnp.zeros_like(total)

    for d, ref in enumerate((v0, v1, v2, v3)):

        @pl.when(step == d)
        def _(ref=ref):
            act[...] = ref[slot * tokens : (slot + 1) * tokens, :]
            held[:half, :] = ref[2 * tokens :, :]

    held[half:, :] = other[0]

    def body(e, _):
        cols = pl.ds(pl.multiple_of(e * width, width), width)
        for k, inv in enumerate((inv0, inv1)):
            here = slice(k * n, (k + 1) * n)
            contracted = dot(flipped[here, :], act[:, cols])
            scaled = (contracted * inv[:, cols]).astype(BF)
            total[here, :] += dot_t(scaled, held[:, cols])
        return 0

    lax.fori_loop(0, 4, body, 0)

    @pl.when(step == pl.num_programs(0) - 1)
    def _():
        out[0:1, :] = (total[...] * query[...]).sum(0, keepdims=True)


def score(slot, at, keep, got, acts, other, inv0, inv1, query):
    tokens, both = keep.shape
    n = inv0.shape[0]
    cols = acts[0].shape[1]
    half = other.shape[1]
    rows = 2 * half

    def whole(a):
        return pl.BlockSpec(a.shape, lambda j, at: (0,) * a.ndim)

    spec = pltpu.PrefetchScalarGridSpec(
        num_scalar_prefetch=1,
        grid=(4,),
        in_specs=[whole(keep), whole(got)]
        + [whole(a) for a in acts]
        + [
            pl.BlockSpec((1, half, cols), lambda j, at: (j, 0, 0)),
            pl.BlockSpec((n, cols), lambda j, at: (0, lax.rem(at[0] + j, 4))),
            pl.BlockSpec((n, cols), lambda j, at: (0, lax.rem(at[0] + j, 4))),
            whole(query),
        ],
        out_specs=pl.BlockSpec((8, rows), lambda j, at: (0, 0)),
        scratch_shapes=[
            pltpu.VMEM((both, tokens), BF),
            pltpu.VMEM((both, rows), F32),
            pltpu.VMEM((tokens, cols), BF),
            pltpu.VMEM((rows, cols), BF),
        ],
    )
    return pl.pallas_call(
        functools.partial(score_kernel, slot),
        grid_spec=spec,
        out_shape=jax.ShapeDtypeStruct((8, rows), F32),
        cost_estimate=pl.CostEstimate(
            flops=2 * both * 4 * cols * (tokens + rows),
            bytes_accessed=4 * both * 4 * cols,
            transcendentals=0,
        ),
    )(at, keep, got, *acts, other, inv0, inv1, query)[0]


def shards(grad_out, act_in, basis_out, basis_in, eigen_vals, query_out, query_in):
    yi, zi, ci, li = (lax.axis_index(a) for a in ("y", "zh", "c", "zl"))
    tokens, unit = grad_out.shape[1:]
    queries, rank = query_out.shape[:2]
    rows = queries * rank
    half_rows = rows // 2
    width = basis_out.shape[1]
    first = ci == 0

    same = li == zi % 2
    at = jnp.stack([yi, zi, ci]).astype(jnp.int32)

    out_t = basis_out.T
    out_both = jnp.concatenate([out_t, shift(out_t, "c", 1)], 0)
    out_both = lax.optimization_barrier(out_both)
    eigen_other = shift(eigen_vals, "c", 1)
    inv0 = 1.0 / eigen_vals.astype(F32)
    inv1 = 1.0 / eigen_other.astype(F32)

    mine = lax.dynamic_slice_in_dim(query_out.reshape(rows, unit), ci * half_rows, half_rows, 0)
    mine_in = lax.dynamic_slice_in_dim(query_in.reshape(rows, -1), ci * half_rows, half_rows, 0)
    in_own = jnp.stack(gather(basis_in, "zh"))
    in_other = shift(in_own, "c", 1)
    part, value = rotate_in(at, gather(act_in[0], "y"), mine_in, (in_own, in_other))
    part = exchange(part.reshape(4, tokens, -1), "x").astype(F32).sum(0).astype(BF)
    part = (part.astype(F32) + to_owner(part).astype(F32)).astype(BF)
    plus, far, minus = (from_owner(part, by) for by in (1, 2, 3))

    query = jnp.concatenate([dot_t(mine, out_both).astype(BF), value], 1)
    some = half_rows // 8
    query = exchange(query.reshape(8, some, -1), ("zl", "x")).reshape(8, some, -1)
    query = query.astype(F32).sum(0).astype(BF)
    query = spread(query, ("zl", "x"), 8).reshape(half_rows, -1)
    value = query[:, 2 * width :]
    query = query[:, : 2 * width]
    swapped = jnp.concatenate([query[:, width:], query[:, :width]], 1)
    query = jnp.concatenate([query, shift(swapped, "c", 1)], 0)
    query_rot = query.astype(F32).T

    act_rot = jnp.concatenate(
        [jnp.where(same, part, minus), jnp.where(same, far, plus), value], 0
    )
    act_rot = gather(act_rot, "y")
    value_other = shift(jnp.stack([a[2 * tokens :] for a in act_rot]), "c", 1)

    grad = grad_out[0]
    plus, far, minus = (shift(grad, "zh", -by) for by in (1, 2, 3))
    blocks = []
    for some_blocks in ((grad,), (plus, minus), (far,)):
        some_blocks = jnp.stack(some_blocks)
        found = lax.all_gather(some_blocks, "y", axis=0, tiled=True)
        product = dot_t(found.reshape(-1, unit), out_both).astype(BF)
        product = exchange(product.reshape(-1, tokens, 2 * width), "x")
        blocks.append(product.reshape(4, -1, tokens, 2 * width))
    flag = same.astype(jnp.int32)[None]
    result = []
    for slot, (a, b, keeps) in enumerate(
        (((blocks[0], 0), (blocks[1], 1), flag), ((blocks[2], 0), (blocks[1], 0), flag))
    ):
        keep, give = split(keeps, a, b)
        got = shift(give, "zl", 1)
        result.append(
            score(slot, at, keep, got, act_rot, value_other, inv0, inv1, query_rot)
        )
    result = jnp.stack(result)
    low = jnp.where(same, zi, (zi + 3) % 4) // 2

    result = result.reshape(2, queries, rank).sum(-1)
    result = jnp.where(low == 0, result, result[::-1])
    turned = jnp.concatenate([result[:, queries // 2 :], result[:, : queries // 2]], 1)
    result = jnp.where(first, result, turned)
    result = spread(result, ("y", "zh"), 16).reshape(16, 2, queries).sum(0)
    result = spread(result, ("c", "zl", "x"), 16).reshape(2, 2, 4, 2, queries)
    result = result.transpose(2, 3, 1, 0, 4).reshape(8, 4, queries)
    return lax.dynamic_index_in_dim(result, li * 4 + lax.axis_index("x"), 0, False)


def solution(mesh):
    fine = Mesh(mesh.devices.reshape(SIZES), AXES)
    dp, factor = ("y", "zh", "c"), ("zl", "x")
    in_specs = (
        P(dp, None, factor),
        P(dp, None, factor),
        P(factor, dp),
        P(factor, dp),
        P(dp, None),
        P(None, None, factor),
        P(None, None, factor),
    )

    return jax.shard_map(
        shards, mesh=fine, in_specs=in_specs, out_specs=P(factor, None), check_vma=False
    )
```

```python
import functools

import jax
import jax.numpy as jnp
from jax import lax
from jax.experimental import pallas as pl
from jax.experimental.pallas import tpu as pltpu
from jax.sharding import Mesh, PartitionSpec as P


AXES = ("y", "zh", "c", "zl", "x")
SIZES = (4, 4, 2, 2, 4)
BF = jnp.bfloat16
F32 = jnp.float32


def shift(value, axis, by):
    n = SIZES[AXES.index(axis)]
    return lax.ppermute(value, axis, [(i, (i + by) % n) for i in range(n)])


def gather(value, axis):
    return [value] + [shift(value, axis, -by) for by in (1, 2, 3)]


def from_owner(value, by):
    pairs = [(2 * h + h % 2, 2 * ((h - by) % 4) + h % 2) for h in range(4)]
    return lax.ppermute(value, ("zh", "zl"), pairs)


def to_owner(value):
    pairs = [(2 * h + 1 - h % 2, 2 * h + h % 2) for h in range(4)]
    return lax.ppermute(value, ("zh", "zl"), pairs)


def exchange(value, axes):
    return lax.all_to_all(value, axes, 0, 0, tiled=True)


def spread(value, axes, n):
    return exchange(jnp.broadcast_to(value[None], (n,) + value.shape), axes)


def dot(a, b):
    return jnp.dot(a, b, preferred_element_type=F32)


def dot_t(a, b):
    return lax.dot_general(a, b, (((1,), (1,)), ((), ())), preferred_element_type=F32)


def rotate_in_kernel(at_ref, a0, a1, a2, a3, q, w0, w1, out, value, act):
    tokens = a0.shape[0]
    n = w0.shape[2]
    for d, a in enumerate((a0, a1, a2, a3)):
        y = lax.rem(at_ref[0] + d, 4)
        act[pl.ds(pl.multiple_of(y * tokens, tokens), tokens), :] = a[...]
    act[4 * tokens :, :] = q[...]
    for k, w in enumerate((w0, w1)):
        core = at_ref[2] if k == 0 else 1 - at_ref[2]
        for d in range(4):
            zh = lax.rem(at_ref[1] + d, 4)
            here = pl.ds(pl.multiple_of((2 * zh + core) * n, n), n)
            product = dot(act[...], w[d]).astype(BF)
            out[:, here] = product[: 4 * tokens]
            value[:, here] = product[4 * tokens :]


def rotate_in(at, acts, query, bases):
    tokens, unit = acts[0].shape
    rows = query.shape[0]
    n = bases[0].shape[2]
    vmem = pl.BlockSpec(memory_space=pltpu.VMEM)
    return pl.pallas_call(
        rotate_in_kernel,
        in_specs=[pl.BlockSpec(memory_space=pltpu.SMEM)] + [vmem] * 7,
        out_specs=(vmem, vmem),
        out_shape=(
            jax.ShapeDtypeStruct((4 * tokens, 8 * n), BF),
            jax.ShapeDtypeStruct((rows, 8 * n), BF),
        ),
        scratch_shapes=[pltpu.VMEM((4 * tokens + rows, unit), BF)],
        cost_estimate=pl.CostEstimate(
            flops=2 * 32 * tokens * unit * n, bytes_accessed=2 * 16 * tokens * (unit + n), transcendentals=0
        ),
        name="rotate_in",
    )(at, *acts, query, *bases)


def split_kernel(at_ref, *refs):
    keep, give = refs[8:]

    def total(refs):
        own = refs[0][0, 0].astype(F32)
        return sum((r[0].astype(F32) for r in refs[1:]), own).astype(BF)

    @pl.when(at_ref[3] == 1)
    def _():
        keep[...] = total(refs[:4])
        give[...] = total(refs[4:8])

    @pl.when(at_ref[3] == 0)
    def _():
        keep[...] = total(refs[4:8])
        give[...] = total(refs[:4])


def split(at, a, b):
    tokens, both = a[0][0].shape[2:]
    tile = tokens // 2
    specs = []
    for parts, which in (a, b):
        specs.append(pl.BlockSpec((1, 1, tile, both), lambda t, at, w=which: (at[4], w, t, 0)))
        specs += [pl.BlockSpec((1, tile, both), lambda t, at, w=which: (w, t, 0))] * 3
    out = pl.BlockSpec((tile, both), lambda t, at: (t, 0))
    shape = jax.ShapeDtypeStruct((tokens, both), BF)
    spec = pltpu.PrefetchScalarGridSpec(
        num_scalar_prefetch=1, grid=(2,), in_specs=specs, out_specs=(out, out)
    )
    return pl.pallas_call(
        split_kernel,
        grid_spec=spec,
        out_shape=(shape, shape),
        cost_estimate=pl.CostEstimate(
            flops=8 * tokens * both, bytes_accessed=20 * tokens * both, transcendentals=0
        ),
    )(at, *a[0], *b[0])


def score_kernel(slot, at_ref, keep, got, v0, v1, v2, v3, other, inv0, inv1, query, out, flipped, total, act, held):
    step = pl.program_id(0)
    n = inv0.shape[0]
    tokens = keep.shape[0]
    half = other.shape[1]
    width = act.shape[1] // 4

    @pl.when(step == 0)
    def _():
        grad = keep[...].astype(F32) + got[...].astype(F32)
        flipped[...] = grad.T.astype(BF)
        total[...] = jnp.zeros_like(total)

    for d, ref in enumerate((v0, v1, v2, v3)):

        @pl.when(step == d)
        def _(ref=ref):
            act[...] = ref[slot * tokens : (slot + 1) * tokens, :]
            held[:half, :] = ref[2 * tokens :, :]

    held[half:, :] = other[0]

    def body(e):
        cols = slice(e * width, (e + 1) * width)
        for k, inv in enumerate((inv0, inv1)):
            here = slice(k * n, (k + 1) * n)
            contracted = dot(flipped[here, :], act[:, cols])
            scaled = (contracted * inv[:, cols]).astype(BF)
            total[here, :] += dot_t(scaled, held[:, cols])

    for e in range(4):
        body(e)

    @pl.when(step == pl.num_programs(0) - 1)
    def _():
        out[0:1, :] = (total[...] * query[...]).sum(0, keepdims=True)


def score(slot, at, keep, got, acts, other, inv0, inv1, query):
    tokens, both = keep.shape
    n = inv0.shape[0]
    cols = acts[0].shape[1]
    half = other.shape[1]
    rows = 2 * half

    def whole(a):
        return pl.BlockSpec(a.shape, lambda j, at: (0,) * a.ndim)

    spec = pltpu.PrefetchScalarGridSpec(
        num_scalar_prefetch=1,
        grid=(4,),
        in_specs=[whole(keep), whole(got)]
        + [whole(a) for a in acts]
        + [
            pl.BlockSpec((1, half, cols), lambda j, at: (j, 0, 0)),
            pl.BlockSpec((n, cols), lambda j, at: (0, lax.rem(at[0] + j, 4))),
            pl.BlockSpec((n, cols), lambda j, at: (0, lax.rem(at[0] + j, 4))),
            whole(query),
        ],
        out_specs=pl.BlockSpec((8, rows), lambda j, at: (0, 0)),
        scratch_shapes=[
            pltpu.VMEM((both, tokens), BF),
            pltpu.VMEM((both, rows), F32),
            pltpu.VMEM((tokens, cols), BF),
            pltpu.VMEM((rows, cols), BF),
        ],
    )
    return pl.pallas_call(
        functools.partial(score_kernel, slot),
        grid_spec=spec,
        out_shape=jax.ShapeDtypeStruct((8, rows), F32),
        cost_estimate=pl.CostEstimate(
            flops=2 * both * 4 * cols * (tokens + rows),
            bytes_accessed=4 * both * 4 * cols,
            transcendentals=0,
        ),
    )(at, keep, got, *acts, other, inv0, inv1, query)[0]


def shards(grad_out, act_in, basis_out, basis_in, eigen_vals, query_out, query_in):
    yi, zi, ci, li = (lax.axis_index(a) for a in ("y", "zh", "c", "zl"))
    tokens, unit = grad_out.shape[1:]
    queries, rank = query_out.shape[:2]
    rows = queries * rank
    half_rows = rows // 2
    width = basis_out.shape[1]
    first = ci == 0

    same = li == zi % 2
    xi = lax.axis_index("x")
    at = jnp.stack([yi, zi, ci, same, xi]).astype(jnp.int32)

    out_t = basis_out.T
    out_both = jnp.concatenate([out_t, shift(out_t, "c", 1)], 0)
    out_both = lax.optimization_barrier(out_both)
    eigen_other = shift(eigen_vals, "c", 1)
    inv0 = 1.0 / eigen_vals.astype(F32)
    inv1 = 1.0 / eigen_other.astype(F32)

    mine = lax.dynamic_slice_in_dim(query_out.reshape(rows, unit), ci * half_rows, half_rows, 0)
    mine_in = lax.dynamic_slice_in_dim(query_in.reshape(rows, -1), ci * half_rows, half_rows, 0)
    in_own = jnp.stack(gather(basis_in, "zh"))
    in_other = shift(in_own, "c", 1)
    part, value = rotate_in(at, gather(act_in[0], "y"), mine_in, (in_own, in_other))
    part = exchange(part.reshape(4, tokens, -1), "x").astype(F32).sum(0).astype(BF)
    part = (part.astype(F32) + to_owner(part).astype(F32)).astype(BF)
    plus, far, minus = (from_owner(part, by) for by in (1, 2, 3))

    query = jnp.concatenate([dot_t(mine, out_both).astype(BF), value], 1)
    some = half_rows // 8
    query = exchange(query.reshape(8, some, -1), ("zl", "x")).reshape(8, some, -1)
    query = query.astype(F32).sum(0).astype(BF)
    query = spread(query, ("zl", "x"), 8).reshape(half_rows, -1)
    value = query[:, 2 * width :]
    query = query[:, : 2 * width]
    swapped = jnp.concatenate([query[:, width:], query[:, :width]], 1)
    query = jnp.concatenate([query, shift(swapped, "c", 1)], 0)
    query_rot = query.astype(F32).T

    act_rot = jnp.concatenate(
        [jnp.where(same, part, minus), jnp.where(same, far, plus), value], 0
    )
    act_rot = gather(act_rot, "y")
    value_other = shift(jnp.stack([a[2 * tokens :] for a in act_rot]), "c", 1)

    grad = grad_out[0]
    plus, far, minus = (shift(grad, "zh", -by) for by in (1, 2, 3))
    blocks = []
    for some_blocks in ((grad,), (plus, minus), (far,)):
        some_blocks = jnp.stack(some_blocks)
        found = lax.all_gather(some_blocks, "y", axis=0, tiled=True)
        product = dot_t(found.reshape(-1, unit), out_both).astype(BF)
        product = product.reshape(4, -1, tokens, 2 * width)
        parts = [product]
        for by in (1, 2, 3):
            part = lax.dynamic_index_in_dim(product, (xi + by) % 4, 0, False)
            parts.append(shift(part, "x", by))
        blocks.append(parts)
    result = []
    for slot, (a, b) in enumerate(
        (((blocks[0], 0), (blocks[1], 1)), ((blocks[2], 0), (blocks[1], 0)))
    ):
        keep, give = split(at, a, b)
        got = shift(give, "zl", 1)
        result.append(
            score(slot, at, keep, got, act_rot, value_other, inv0, inv1, query_rot)
        )
    result = jnp.stack(result)
    low = jnp.where(same, zi, (zi + 3) % 4) // 2

    result = result.reshape(2, queries, rank).sum(-1)
    result = jnp.where(low == 0, result, result[::-1])
    turned = jnp.concatenate([result[:, queries // 2 :], result[:, : queries // 2]], 1)
    result = jnp.where(first, result, turned)
    result = spread(result, ("y", "zh"), 16).reshape(16, 2, queries).sum(0)
    result = spread(result, ("c", "zl", "x"), 16).reshape(2, 2, 4, 2, queries)
    result = result.transpose(2, 3, 1, 0, 4).reshape(8, 4, queries)
    return lax.dynamic_index_in_dim(result, li * 4 + lax.axis_index("x"), 0, False)


def solution(mesh):
    fine = Mesh(mesh.devices.reshape(SIZES), AXES)
    dp, factor = ("y", "zh", "c"), ("zl", "x")
    in_specs = (
        P(dp, None, factor),
        P(dp, None, factor),
        P(factor, dp),
        P(factor, dp),
        P(dp, None),
        P(None, None, factor),
        P(None, None, factor),
    )

    return jax.shard_map(
        shards, mesh=fine, in_specs=in_specs, out_specs=P(factor, None), check_vma=False
    )
```

```python
import jax
import jax.numpy as jnp
from jax import lax
from jax.experimental import pallas as pl
from jax.experimental.pallas import tpu as pltpu
from jax.sharding import Mesh, PartitionSpec as P


AXES = ("y", "zh", "c", "zl", "x")
SIZES = (4, 4, 2, 2, 4)
BF = jnp.bfloat16
F32 = jnp.float32


def shift(value, axis, by):
    n = SIZES[AXES.index(axis)]
    return lax.ppermute(value, axis, [(i, (i + by) % n) for i in range(n)])


def gather(value, axis):
    return [value] + [shift(value, axis, -by) for by in (1, 2, 3)]


def from_owner(value, by):
    pairs = [(2 * h + h % 2, 2 * ((h - by) % 4) + h % 2) for h in range(4)]
    return lax.ppermute(value, ("zh", "zl"), pairs)


def to_owner(value):
    pairs = [(2 * h + 1 - h % 2, 2 * h + h % 2) for h in range(4)]
    return lax.ppermute(value, ("zh", "zl"), pairs)


def exchange(value, axes):
    return lax.all_to_all(value, axes, 0, 0, tiled=True)


def spread(value, axes, n):
    return exchange(jnp.broadcast_to(value[None], (n,) + value.shape), axes)


def dot(a, b):
    return jnp.dot(a, b, preferred_element_type=F32)


def dot_t(a, b):
    return lax.dot_general(a, b, (((1,), (1,)), ((), ())), preferred_element_type=F32)


def rotate_in_kernel(at_ref, a0, a1, a2, a3, q, w0, w1, p0, p1, p2, p3, value, act):
    tokens = a0.shape[0]
    n = w0.shape[2]
    for d, a in enumerate((a0, a1, a2, a3)):
        far = lax.rem(at_ref[0] + d + 4 - at_ref[4], 4)
        act[pl.ds(pl.multiple_of(far * tokens, tokens), tokens), :] = a[...]
    act[4 * tokens :, :] = q[...]
    for k, w in enumerate((w0, w1)):
        core = at_ref[2] if k == 0 else 1 - at_ref[2]
        for d in range(4):
            zh = lax.rem(at_ref[1] + d, 4)
            here = pl.ds(pl.multiple_of((2 * zh + core) * n, n), n)
            product = dot(act[...], w[d]).astype(BF)
            for e, out in enumerate((p0, p1, p2, p3)):
                out[:, here] = product[e * tokens : (e + 1) * tokens]
            value[:, here] = product[4 * tokens :]


def rotate_in(at, acts, query, bases):
    tokens, unit = acts[0].shape
    rows = query.shape[0]
    n = bases[0].shape[2]
    vmem = pl.BlockSpec(memory_space=pltpu.VMEM)
    return pl.pallas_call(
        rotate_in_kernel,
        in_specs=[pl.BlockSpec(memory_space=pltpu.SMEM)] + [vmem] * 7,
        out_specs=(vmem,) * 5,
        out_shape=(jax.ShapeDtypeStruct((tokens, 8 * n), BF),) * 4
        + (jax.ShapeDtypeStruct((rows, 8 * n), BF),),
        scratch_shapes=[pltpu.VMEM((4 * tokens + rows, unit), BF)],
        cost_estimate=pl.CostEstimate(
            flops=2 * 32 * tokens * unit * n, bytes_accessed=2 * 16 * tokens * (unit + n), transcendentals=0
        ),
        name="rotate_in",
    )(at, *acts, query, *bases)


def split_kernel(at_ref, *refs):
    keep, give = refs[8:]

    def total(refs):
        own = refs[0][0, 0].astype(F32)
        return sum((r[0].astype(F32) for r in refs[1:]), own).astype(BF)

    @pl.when(at_ref[3] == 1)
    def _():
        keep[...] = total(refs[:4])
        give[...] = total(refs[4:8])

    @pl.when(at_ref[3] == 0)
    def _():
        keep[...] = total(refs[4:8])
        give[...] = total(refs[:4])


def split(at, a, b):
    tokens, both = a[0][0].shape[2:]
    tile = tokens // 2
    specs = []
    for parts, which in (a, b):
        specs.append(pl.BlockSpec((1, 1, tile, both), lambda t, at, w=which: (at[4], w, t, 0)))
        specs += [pl.BlockSpec((1, tile, both), lambda t, at, w=which: (w, t, 0))] * 3
    out = pl.BlockSpec((tile, both), lambda t, at: (t, 0))
    shape = jax.ShapeDtypeStruct((tokens, both), BF)
    spec = pltpu.PrefetchScalarGridSpec(
        num_scalar_prefetch=1, grid=(2,), in_specs=specs, out_specs=(out, out)
    )
    return pl.pallas_call(
        split_kernel,
        grid_spec=spec,
        out_shape=(shape, shape),
        cost_estimate=pl.CostEstimate(
            flops=8 * tokens * both, bytes_accessed=20 * tokens * both, transcendentals=0
        ),
    )(at, *a[0], *b[0])


def score_kernel(
    at_ref, k0, k1, g0, g1, v0, v1, v2, v3, other, inv0, inv1, query, out, flipped, total, act, held
):
    step = pl.program_id(0)
    n = inv0.shape[0]
    tokens = k0.shape[0]
    half = other.shape[1]
    cols = inv0.shape[1]
    width = cols // 2

    @pl.when(step == 0)
    def _():
        for s, (keep, got) in enumerate(((k0, g0), (k1, g1))):
            grad = keep[...].astype(F32) + got[...].astype(F32)
            flipped[s] = grad.T.astype(BF)
        total[...] = jnp.zeros_like(total)

    for d, ref in enumerate((v0, v1, v2, v3)):

        @pl.when(step // 2 == d)
        def _(ref=ref):
            here = pl.ds(pl.multiple_of(lax.rem(step, 2) * cols, cols), cols)
            act[...] = ref[: 2 * tokens, here]
            held[:half, :] = ref[2 * tokens :, here]

    held[half:, :] = other[0]
    for e in range(2):
        here = slice(e * width, (e + 1) * width)
        for k, inv in enumerate((inv0, inv1)):
            lines = slice(k * n, (k + 1) * n)
            for s in range(2):
                contracted = dot(flipped[s, lines, :], act[s * tokens : (s + 1) * tokens, here])
                scaled = (contracted * inv[:, here]).astype(BF)
                total[s, lines, :] += dot_t(scaled, held[:, here])

    @pl.when(step == pl.num_programs(0) - 1)
    def _():
        for s in range(2):
            out[s : s + 1, :] = (total[s] * query[...]).sum(0, keepdims=True)


def score(at, grads, acts, other, inv0, inv1, query):
    tokens, both = grads[0].shape
    n = inv0.shape[0]
    cols = acts[0].shape[1] // 2
    half = other.shape[1]
    rows = 2 * half

    def whole(a):
        return pl.BlockSpec(a.shape, lambda j, at: (0,) * a.ndim)

    def strip(j, at):
        return (0, 2 * lax.rem(at[0] + j // 2, 4) + lax.rem(j, 2))

    spec = pltpu.PrefetchScalarGridSpec(
        num_scalar_prefetch=1,
        grid=(8,),
        in_specs=[whole(a) for a in (*grads, *acts)]
        + [
            pl.BlockSpec((1, half, cols), lambda j, at: (j // 2, 0, lax.rem(j, 2))),
            pl.BlockSpec((n, cols), strip),
            pl.BlockSpec((n, cols), strip),
            whole(query),
        ],
        out_specs=pl.BlockSpec((8, rows), lambda j, at: (0, 0)),
        scratch_shapes=[
            pltpu.VMEM((2, both, tokens), BF),
            pltpu.VMEM((2, both, rows), F32),
            pltpu.VMEM((2 * tokens, cols), BF),
            pltpu.VMEM((rows, cols), BF),
        ],
    )
    return pl.pallas_call(
        score_kernel,
        grid_spec=spec,
        out_shape=jax.ShapeDtypeStruct((8, rows), F32),
        cost_estimate=pl.CostEstimate(
            flops=2 * 2 * both * 8 * cols * (tokens + rows),
            bytes_accessed=4 * both * 8 * cols,
            transcendentals=0,
        ),
        name="score",
    )(at, *grads, *acts, other, inv0, inv1, query)[:2]


def shards(grad_out, act_in, basis_out, basis_in, eigen_vals, query_out, query_in):
    yi, zi, ci, li = (lax.axis_index(a) for a in ("y", "zh", "c", "zl"))
    tokens, unit = grad_out.shape[1:]
    queries, rank = query_out.shape[:2]
    rows = queries * rank
    half_rows = rows // 2
    width = basis_out.shape[1]
    first = ci == 0

    same = li == zi % 2
    xi = lax.axis_index("x")
    at = jnp.stack([yi, zi, ci, same, xi]).astype(jnp.int32)

    out_t = basis_out.T
    out_both = jnp.concatenate([out_t, shift(out_t, "c", 1)], 0)
    out_both = lax.optimization_barrier(out_both)
    eigen_other = shift(eigen_vals, "c", 1)
    inv0 = 1.0 / eigen_vals.astype(F32)
    inv1 = 1.0 / eigen_other.astype(F32)

    mine = lax.dynamic_slice_in_dim(query_out.reshape(rows, unit), ci * half_rows, half_rows, 0)
    mine_in = lax.dynamic_slice_in_dim(query_in.reshape(rows, -1), ci * half_rows, half_rows, 0)
    in_own = jnp.stack(gather(basis_in, "zh"))
    in_other = shift(in_own, "c", 1)
    *parts, value = rotate_in(at, gather(act_in[0], "y"), mine_in, (in_own, in_other))
    part = parts[0].astype(F32)
    for by in (1, 2, 3):
        part = part + shift(parts[by], "x", by).astype(F32)
    part = part.astype(BF)
    part = (part.astype(F32) + to_owner(part).astype(F32)).astype(BF)
    plus, far, minus = (from_owner(part, by) for by in (1, 2, 3))

    query = dot_t(mine, out_both).astype(BF)
    query = jnp.concatenate([query, value], 1)
    some = half_rows // 8
    query = exchange(query.reshape(8, some, -1), ("zl", "x")).reshape(8, some, -1)
    query = query.astype(F32).sum(0).astype(BF)
    query = spread(query, ("zl", "x"), 8).reshape(half_rows, -1)
    value = query[:, 2 * width :]
    query = query[:, : 2 * width]
    swapped = jnp.concatenate([query[:, width:], query[:, :width]], 1)
    query = jnp.concatenate([query, shift(swapped, "c", 1)], 0)
    query_rot = query.astype(F32).T

    act_rot = jnp.concatenate(
        [jnp.where(same, part, minus), jnp.where(same, far, plus), value], 0
    )
    act_rot = gather(act_rot, "y")
    value_other = shift(jnp.stack([a[2 * tokens :] for a in act_rot]), "c", 1)

    grad = grad_out[0]
    plus, far, minus = (shift(grad, "zh", -by) for by in (1, 2, 3))
    blocks = []
    for some_blocks in ((grad,), (plus, minus), (far,)):
        some_blocks = jnp.stack(some_blocks)
        found = lax.all_gather(some_blocks, "y", axis=0, tiled=True)
        product = dot_t(found.reshape(-1, unit), out_both).astype(BF)
        product = product.reshape(4, -1, tokens, 2 * width)
        parts = [product]
        for by in (1, 2, 3):
            part = lax.dynamic_index_in_dim(product, (xi + by) % 4, 0, False)
            parts.append(shift(part, "x", by))
        blocks.append(parts)
    keeps, gots = [], []
    for a, b in (((blocks[0], 0), (blocks[1], 1)), ((blocks[2], 0), (blocks[1], 0))):
        keep, give = split(at, a, b)
        keeps.append(keep)
        gots.append(shift(give, "zl", 1))
    result = score(at, (*keeps, *gots), act_rot, value_other, inv0, inv1, query_rot)
    low = jnp.where(same, zi, (zi + 3) % 4) // 2

    result = result.reshape(2, queries, rank).sum(-1)
    result = jnp.where(low == 0, result, result[::-1])
    turned = jnp.concatenate([result[:, queries // 2 :], result[:, : queries // 2]], 1)
    result = jnp.where(first, result, turned)
    result = spread(result, ("y", "zh"), 16).reshape(16, 2, queries).sum(0)
    result = spread(result, ("c", "zl", "x"), 16).reshape(2, 2, 4, 2, queries)
    result = result.transpose(2, 3, 1, 0, 4).reshape(8, 4, queries)
    return lax.dynamic_index_in_dim(result, li * 4 + lax.axis_index("x"), 0, False)


def solution(mesh):
    fine = Mesh(mesh.devices.reshape(SIZES), AXES)
    dp, factor = ("y", "zh", "c"), ("zl", "x")
    in_specs = (
        P(dp, None, factor),
        P(dp, None, factor),
        P(factor, dp),
        P(factor, dp),
        P(dp, None),
        P(None, None, factor),
        P(None, None, factor),
    )

    return jax.shard_map(
        shards, mesh=fine, in_specs=in_specs, out_specs=P(factor, None), check_vma=False
    )
```

```python
import jax
import jax.numpy as jnp
from jax import lax
from jax.experimental import pallas as pl
from jax.experimental.pallas import tpu as pltpu
from jax.sharding import Mesh, PartitionSpec as P


AXES = ("y", "zh", "c", "zl", "x")
SIZES = (4, 4, 2, 2, 4)
BF = jnp.bfloat16
F32 = jnp.float32


def shift(value, axis, by):
    n = SIZES[AXES.index(axis)]
    return lax.ppermute(value, axis, [(i, (i + by) % n) for i in range(n)])


def gather(value, axis):
    return [value] + [shift(value, axis, -by) for by in (1, 2, 3)]


def from_owner(value, by):
    pairs = [(2 * h + h % 2, 2 * ((h - by) % 4) + h % 2) for h in range(4)]
    return lax.ppermute(value, ("zh", "zl"), pairs)


def to_owner(value):
    pairs = [(2 * h + 1 - h % 2, 2 * h + h % 2) for h in range(4)]
    return lax.ppermute(value, ("zh", "zl"), pairs)


def exchange(value, axes):
    return lax.all_to_all(value, axes, 0, 0, tiled=True)


def spread(value, axes, n):
    return exchange(jnp.broadcast_to(value[None], (n,) + value.shape), axes)


def dot(a, b):
    return jnp.dot(a, b, preferred_element_type=F32)


def dot_t(a, b):
    return lax.dot_general(a, b, (((1,), (1,)), ((), ())), preferred_element_type=F32)


def rotate_in_kernel(at_ref, a0, a1, a2, a3, q, w0, w1, p0, p1, p2, p3, value, act):
    tokens = a0.shape[0]
    n = w0.shape[2]
    for d, a in enumerate((a0, a1, a2, a3)):
        far = lax.rem(at_ref[0] + d + 4 - at_ref[4], 4)
        act[pl.ds(pl.multiple_of(far * tokens, tokens), tokens), :] = a[...]
    act[4 * tokens :, :] = q[...]
    for k, w in enumerate((w0, w1)):
        core = at_ref[2] if k == 0 else 1 - at_ref[2]
        for d in range(4):
            zh = lax.rem(at_ref[1] + d, 4)
            here = pl.ds(pl.multiple_of((2 * zh + core) * n, n), n)
            product = dot(act[...], w[d]).astype(BF)
            for e, out in enumerate((p0, p1, p2, p3)):
                out[:, here] = product[e * tokens : (e + 1) * tokens]
            value[:, here] = product[4 * tokens :]


def rotate_in(at, acts, query, bases):
    tokens, unit = acts[0].shape
    rows = query.shape[0]
    n = bases[0].shape[2]
    vmem = pl.BlockSpec(memory_space=pltpu.VMEM)
    return pl.pallas_call(
        rotate_in_kernel,
        in_specs=[pl.BlockSpec(memory_space=pltpu.SMEM)] + [vmem] * 7,
        out_specs=(vmem,) * 5,
        out_shape=(jax.ShapeDtypeStruct((tokens, 8 * n), BF),) * 4
        + (jax.ShapeDtypeStruct((rows, 8 * n), BF),),
        scratch_shapes=[pltpu.VMEM((4 * tokens + rows, unit), BF)],
        cost_estimate=pl.CostEstimate(
            flops=2 * 32 * tokens * unit * n, bytes_accessed=2 * 16 * tokens * (unit + n), transcendentals=0
        ),
        name="rotate_in",
    )(at, *acts, query, *bases)


def split_kernel(at_ref, *refs):
    keep, give = refs[8:]

    def total(refs):
        own = refs[0][0, 0].astype(F32)
        return sum((r[0].astype(F32) for r in refs[1:]), own).astype(BF)

    @pl.when(at_ref[3] == 1)
    def _():
        keep[...] = total(refs[:4])
        give[...] = total(refs[4:8])

    @pl.when(at_ref[3] == 0)
    def _():
        keep[...] = total(refs[4:8])
        give[...] = total(refs[:4])


def split(at, a, b):
    tokens, both = a[0][0].shape[2:]
    tile = tokens // 2
    specs = []
    for parts, which in (a, b):
        specs.append(pl.BlockSpec((1, 1, tile, both), lambda t, at, w=which: (at[4], w, t, 0)))
        specs += [pl.BlockSpec((1, tile, both), lambda t, at, w=which: (w, t, 0))] * 3
    out = pl.BlockSpec((tile, both), lambda t, at: (t, 0))
    shape = jax.ShapeDtypeStruct((tokens, both), BF)
    spec = pltpu.PrefetchScalarGridSpec(
        num_scalar_prefetch=1, grid=(2,), in_specs=specs, out_specs=(out, out)
    )
    return pl.pallas_call(
        split_kernel,
        grid_spec=spec,
        out_shape=(shape, shape),
        cost_estimate=pl.CostEstimate(
            flops=8 * tokens * both, bytes_accessed=20 * tokens * both, transcendentals=0
        ),
    )(at, *a[0], *b[0])


def score_kernel(
    at_ref, k0, k1, g0, g1, v0, v1, va, vb, v3, other, inv0, inv1, query, out, flipped, total, act, held
):
    step = pl.program_id(0)
    n = inv0.shape[0]
    tokens = k0.shape[0]
    half = other.shape[1]
    cols = inv0.shape[1]
    width = cols // 2

    @pl.when(step == 0)
    def _():
        for s, (keep, got) in enumerate(((k0, g0), (k1, g1))):
            grad = keep[...].astype(F32) + got[...].astype(F32)
            flipped[s] = grad.T.astype(BF)
        total[...] = jnp.zeros_like(total)

    strip = pl.ds(pl.multiple_of(lax.rem(step, 2) * cols, cols), cols)
    for d, ref in ((0, v0), (1, v1), (3, v3)):

        @pl.when(step // 2 == d)
        def _(ref=ref):
            act[...] = ref[: 2 * tokens, strip]
            held[:half, :] = ref[2 * tokens :, strip]

    @pl.when(step // 2 == 2)
    def _():
        mid = va.shape[0]
        act[:mid, :] = va[:, strip]
        act[mid:, :] = vb[: 2 * tokens - mid, strip]
        held[:half, :] = vb[2 * tokens - mid :, strip]

    held[half:, :] = other[0]
    for e in range(2):
        here = slice(e * width, (e + 1) * width)
        for k, inv in enumerate((inv0, inv1)):
            lines = slice(k * n, (k + 1) * n)
            for s in range(2):
                contracted = dot(flipped[s, lines, :], act[s * tokens : (s + 1) * tokens, here])
                scaled = (contracted * inv[:, here]).astype(BF)
                total[s, lines, :] += dot_t(scaled, held[:, here])

    @pl.when(step == pl.num_programs(0) - 1)
    def _():
        for s in range(2):
            out[s : s + 1, :] = (total[s] * query[...]).sum(0, keepdims=True)


def score(at, grads, acts, other, inv0, inv1, query):
    tokens, both = grads[0].shape
    n = inv0.shape[0]
    cols = acts[0].shape[1] // 2
    half = other.shape[1]
    rows = 2 * half

    def whole(a):
        return pl.BlockSpec(a.shape, lambda j, at: (0,) * a.ndim)

    def strip(j, at):
        return (0, 2 * lax.rem(at[0] + j // 2, 4) + lax.rem(j, 2))

    spec = pltpu.PrefetchScalarGridSpec(
        num_scalar_prefetch=1,
        grid=(8,),
        in_specs=[whole(a) for a in (*grads, *acts)]
        + [
            pl.BlockSpec((1, half, cols), lambda j, at: (j // 2, 0, lax.rem(j, 2))),
            pl.BlockSpec((n, cols), strip),
            pl.BlockSpec((n, cols), strip),
            whole(query),
        ],
        out_specs=pl.BlockSpec((8, rows), lambda j, at: (0, 0)),
        scratch_shapes=[
            pltpu.VMEM((2, both, tokens), BF),
            pltpu.VMEM((2, both, rows), F32),
            pltpu.VMEM((2 * tokens, cols), BF),
            pltpu.VMEM((rows, cols), BF),
        ],
    )
    return pl.pallas_call(
        score_kernel,
        grid_spec=spec,
        out_shape=jax.ShapeDtypeStruct((8, rows), F32),
        cost_estimate=pl.CostEstimate(
            flops=2 * 2 * both * 8 * cols * (tokens + rows),
            bytes_accessed=4 * both * 8 * cols,
            transcendentals=0,
        ),
        name="score",
    )(at, *grads, *acts, other, inv0, inv1, query)[:2]


def shards(grad_out, act_in, basis_out, basis_in, eigen_vals, query_out, query_in):
    yi, zi, ci, li = (lax.axis_index(a) for a in ("y", "zh", "c", "zl"))
    tokens, unit = grad_out.shape[1:]
    queries, rank = query_out.shape[:2]
    rows = queries * rank
    half_rows = rows // 2
    width = basis_out.shape[1]
    first = ci == 0

    same = li == zi % 2
    xi = lax.axis_index("x")
    at = jnp.stack([yi, zi, ci, same, xi]).astype(jnp.int32)

    out_t = basis_out.T
    out_both = jnp.concatenate([out_t, shift(out_t, "c", 1)], 0)
    out_both = lax.optimization_barrier(out_both)
    eigen_other = shift(eigen_vals, "c", 1)
    inv0 = 1.0 / eigen_vals.astype(F32)
    inv1 = 1.0 / eigen_other.astype(F32)

    mine = lax.dynamic_slice_in_dim(query_out.reshape(rows, unit), ci * half_rows, half_rows, 0)
    mine_in = lax.dynamic_slice_in_dim(query_in.reshape(rows, -1), ci * half_rows, half_rows, 0)
    in_own = jnp.stack(gather(basis_in, "zh"))
    in_other = shift(in_own, "c", 1)
    *parts, value = rotate_in(at, gather(act_in[0], "y"), mine_in, (in_own, in_other))
    part = parts[0].astype(F32)
    for by in (1, 2, 3):
        part = part + shift(parts[by], "x", by).astype(F32)
    part = part.astype(BF)
    part = (part.astype(F32) + to_owner(part).astype(F32)).astype(BF)
    plus, far, minus = (from_owner(part, by) for by in (1, 2, 3))

    query = dot_t(mine, out_both).astype(BF)
    query = jnp.concatenate([query, value], 1)
    some = half_rows // 8
    query = exchange(query.reshape(8, some, -1), ("zl", "x")).reshape(8, some, -1)
    query = query.astype(F32).sum(0).astype(BF)
    query = spread(query, ("zl", "x"), 8).reshape(half_rows, -1)
    value = query[:, 2 * width :]
    query = query[:, : 2 * width]
    swapped = jnp.concatenate([query[:, width:], query[:, :width]], 1)
    query = jnp.concatenate([query, shift(swapped, "c", 1)], 0)
    query_rot = query.astype(F32).T

    act_rot = jnp.concatenate(
        [jnp.where(same, part, minus), jnp.where(same, far, plus), value], 0
    )
    mid = act_rot.shape[0] // 2
    plus, minus = shift(act_rot, "y", -1), shift(act_rot, "y", 1)
    far_a = shift(plus[:mid], "y", -1)
    far_b = shift(minus[mid:], "y", 1)
    value_other = [a[2 * tokens :] for a in (act_rot, plus)]
    value_other += [far_b[2 * tokens - mid :], minus[2 * tokens :]]
    value_other = shift(jnp.stack(value_other), "c", 1)
    act_rot = (act_rot, plus, far_a, far_b, minus)

    grad = grad_out[0]
    plus, far, minus = (shift(grad, "zh", -by) for by in (1, 2, 3))
    blocks = []
    for some_blocks in ((grad,), (plus, minus), (far,)):
        some_blocks = jnp.stack(some_blocks)
        found = lax.all_gather(some_blocks, "y", axis=0, tiled=True)
        product = dot_t(found.reshape(-1, unit), out_both).astype(BF)
        product = product.reshape(4, -1, tokens, 2 * width)
        parts = [product]
        for by in (1, 2, 3):
            part = lax.dynamic_index_in_dim(product, (xi + by) % 4, 0, False)
            parts.append(shift(part, "x", by))
        blocks.append(parts)
    keeps, gots = [], []
    for a, b in (((blocks[0], 0), (blocks[1], 1)), ((blocks[2], 0), (blocks[1], 0))):
        keep, give = split(at, a, b)
        keeps.append(keep)
        gots.append(shift(give, "zl", 1))
    result = score(at, (*keeps, *gots), act_rot, value_other, inv0, inv1, query_rot)
    low = jnp.where(same, zi, (zi + 3) % 4) // 2

    result = result.reshape(2, queries, rank).sum(-1)
    result = jnp.where(low == 0, result, result[::-1])
    turned = jnp.concatenate([result[:, queries // 2 :], result[:, : queries // 2]], 1)
    result = jnp.where(first, result, turned)
    result = spread(result, ("y", "zh"), 16).reshape(16, 2, queries).sum(0)
    result = spread(result, ("c", "zl", "x"), 16).reshape(2, 2, 4, 2, queries)
    result = result.transpose(2, 3, 1, 0, 4).reshape(8, 4, queries)
    return lax.dynamic_index_in_dim(result, li * 4 + lax.axis_index("x"), 0, False)


def solution(mesh):
    fine = Mesh(mesh.devices.reshape(SIZES), AXES)
    dp, factor = ("y", "zh", "c"), ("zl", "x")
    in_specs = (
        P(dp, None, factor),
        P(dp, None, factor),
        P(factor, dp),
        P(factor, dp),
        P(dp, None),
        P(None, None, factor),
        P(None, None, factor),
    )

    return jax.shard_map(
        shards, mesh=fine, in_specs=in_specs, out_specs=P(factor, None), check_vma=False
    )
```

```python
import jax
import jax.numpy as jnp
from jax import lax
from jax.experimental import pallas as pl
from jax.experimental.pallas import tpu as pltpu
from jax.sharding import Mesh, PartitionSpec as P


AXES = ("y", "zh", "c", "zl", "x")
SIZES = (4, 4, 2, 2, 4)
BF = jnp.bfloat16
F32 = jnp.float32


def shift(value, axis, by):
    n = SIZES[AXES.index(axis)]
    return lax.ppermute(value, axis, [(i, (i + by) % n) for i in range(n)])


def gather(value, axis):
    return [value] + [shift(value, axis, -by) for by in (1, 2, 3)]


def from_owner(value, by):
    pairs = [(2 * h + h % 2, 2 * ((h - by) % 4) + h % 2) for h in range(4)]
    return lax.ppermute(value, ("zh", "zl"), pairs)


def to_owner(value):
    pairs = [(2 * h + 1 - h % 2, 2 * h + h % 2) for h in range(4)]
    return lax.ppermute(value, ("zh", "zl"), pairs)


def exchange(value, axes):
    return lax.all_to_all(value, axes, 0, 0, tiled=True)


def spread(value, axes, n):
    return exchange(jnp.broadcast_to(value[None], (n,) + value.shape), axes)


def dot(a, b):
    return jnp.dot(a, b, preferred_element_type=F32)


def dot_t(a, b):
    return lax.dot_general(a, b, (((1,), (1,)), ((), ())), preferred_element_type=F32)


def rotate_in_kernel(at_ref, a0, a1, a2, a3, q, w0, w1, p0, p1, p2, p3, value, act):
    tokens = a0.shape[0]
    n = w0.shape[2]
    for d, a in enumerate((a0, a1, a2, a3)):
        far = lax.rem(at_ref[0] + d + 4 - at_ref[4], 4)
        act[pl.ds(pl.multiple_of(far * tokens, tokens), tokens), :] = a[...]
    act[4 * tokens :, :] = q[...]
    for k, w in enumerate((w0, w1)):
        core = at_ref[2] if k == 0 else 1 - at_ref[2]
        for d in range(4):
            zh = lax.rem(at_ref[1] + d, 4)
            here = pl.ds(pl.multiple_of((2 * zh + core) * n, n), n)
            product = dot(act[...], w[d]).astype(BF)
            for e, out in enumerate((p0, p1, p2, p3)):
                out[:, here] = product[e * tokens : (e + 1) * tokens]
            value[:, here] = product[4 * tokens :]


def rotate_in(at, acts, query, bases):
    tokens, unit = acts[0].shape
    rows = query.shape[0]
    n = bases[0].shape[2]
    vmem = pl.BlockSpec(memory_space=pltpu.VMEM)
    return pl.pallas_call(
        rotate_in_kernel,
        in_specs=[pl.BlockSpec(memory_space=pltpu.SMEM)] + [vmem] * 7,
        out_specs=(vmem,) * 5,
        out_shape=(jax.ShapeDtypeStruct((tokens, 8 * n), BF),) * 4
        + (jax.ShapeDtypeStruct((rows, 8 * n), BF),),
        scratch_shapes=[pltpu.VMEM((4 * tokens + rows, unit), BF)],
        cost_estimate=pl.CostEstimate(
            flops=2 * 32 * tokens * unit * n, bytes_accessed=2 * 16 * tokens * (unit + n), transcendentals=0
        ),
        name="rotate_in",
    )(at, *acts, query, *bases)


def split_kernel(at_ref, *refs):
    keep, give = refs[8:]

    def total(refs):
        own = refs[0][0, 0].astype(F32)
        return sum((r[0].astype(F32) for r in refs[1:]), own).astype(BF)

    @pl.when(at_ref[3] == 1)
    def _():
        keep[...] = total(refs[:4])
        give[...] = total(refs[4:8])

    @pl.when(at_ref[3] == 0)
    def _():
        keep[...] = total(refs[4:8])
        give[...] = total(refs[:4])


def split(at, a, b):
    tokens, both = a[0][0].shape[2:]
    tile = tokens // 2
    specs = []
    for parts, which in (a, b):
        specs.append(pl.BlockSpec((1, 1, tile, both), lambda t, at, w=which: (at[4], w, t, 0)))
        specs += [pl.BlockSpec((1, tile, both), lambda t, at, w=which: (w, t, 0))] * 3
    out = pl.BlockSpec((tile, both), lambda t, at: (t, 0))
    shape = jax.ShapeDtypeStruct((tokens, both), BF)
    spec = pltpu.PrefetchScalarGridSpec(
        num_scalar_prefetch=1, grid=(2,), in_specs=specs, out_specs=(out, out)
    )
    return pl.pallas_call(
        split_kernel,
        grid_spec=spec,
        out_shape=(shape, shape),
        cost_estimate=pl.CostEstimate(
            flops=8 * tokens * both, bytes_accessed=20 * tokens * both, transcendentals=0
        ),
    )(at, *a[0], *b[0])


def pick_kernel(a0, a1, a2, a3, out):
    for d, a in enumerate((a0, a1, a2, a3)):
        out[d] = a[...]


def pick(arrays, rows):
    total, cols = arrays[0].shape
    return pl.pallas_call(
        pick_kernel,
        grid=(1,),
        out_shape=jax.ShapeDtypeStruct((4, rows, cols), BF),
        in_specs=[pl.BlockSpec((rows, cols), lambda j: (total // rows - 1, 0))] * 4,
        out_specs=pl.BlockSpec((4, rows, cols), lambda j: (0, 0, 0)),
        cost_estimate=pl.CostEstimate(
            flops=0, bytes_accessed=16 * rows * cols, transcendentals=0
        ),
        name="pick",
    )(*arrays)


def score_kernel(
    at_ref, k0, k1, g0, g1, v0, v1, v2, v3, other, inv0, inv1, query, out, flipped, total, act, held
):
    step = pl.program_id(0)
    n = inv0.shape[0]
    tokens = k0.shape[0]
    half = other.shape[1]
    cols = inv0.shape[1]
    width = cols // 2

    @pl.when(step == 0)
    def _():
        for s, (keep, got) in enumerate(((k0, g0), (k1, g1))):
            grad = keep[...].astype(F32) + got[...].astype(F32)
            flipped[s] = grad.T.astype(BF)
        total[...] = jnp.zeros_like(total)

    for d, ref in enumerate((v0, v1, v2, v3)):

        @pl.when(step // 2 == d)
        def _(ref=ref):
            here = pl.ds(pl.multiple_of(lax.rem(step, 2) * cols, cols), cols)
            act[...] = ref[: 2 * tokens, here]
            held[:half, :] = ref[2 * tokens :, here]

    held[half:, :] = other[0]
    for e in range(2):
        here = slice(e * width, (e + 1) * width)
        for k, inv in enumerate((inv0, inv1)):
            lines = slice(k * n, (k + 1) * n)
            for s in range(2):
                contracted = dot(flipped[s, lines, :], act[s * tokens : (s + 1) * tokens, here])
                scaled = (contracted * inv[:, here]).astype(BF)
                total[s, lines, :] += dot_t(scaled, held[:, here])

    @pl.when(step == pl.num_programs(0) - 1)
    def _():
        for s in range(2):
            out[s : s + 1, :] = (total[s] * query[...]).sum(0, keepdims=True)


def score(at, grads, acts, other, inv0, inv1, query):
    tokens, both = grads[0].shape
    n = inv0.shape[0]
    cols = acts[0].shape[1] // 2
    half = other.shape[1]
    rows = 2 * half

    def whole(a):
        return pl.BlockSpec(a.shape, lambda j, at: (0,) * a.ndim)

    def strip(j, at):
        return (0, 2 * lax.rem(at[0] + j // 2, 4) + lax.rem(j, 2))

    spec = pltpu.PrefetchScalarGridSpec(
        num_scalar_prefetch=1,
        grid=(8,),
        in_specs=[whole(a) for a in (*grads, *acts)]
        + [
            pl.BlockSpec((1, half, cols), lambda j, at: (j // 2, 0, lax.rem(j, 2))),
            pl.BlockSpec((n, cols), strip),
            pl.BlockSpec((n, cols), strip),
            whole(query),
        ],
        out_specs=pl.BlockSpec((8, rows), lambda j, at: (0, 0)),
        scratch_shapes=[
            pltpu.VMEM((2, both, tokens), BF),
            pltpu.VMEM((2, both, rows), F32),
            pltpu.VMEM((2 * tokens, cols), BF),
            pltpu.VMEM((rows, cols), BF),
        ],
    )
    return pl.pallas_call(
        score_kernel,
        grid_spec=spec,
        out_shape=jax.ShapeDtypeStruct((8, rows), F32),
        cost_estimate=pl.CostEstimate(
            flops=2 * 2 * both * 8 * cols * (tokens + rows),
            bytes_accessed=4 * both * 8 * cols,
            transcendentals=0,
        ),
        name="score",
    )(at, *grads, *acts, other, inv0, inv1, query)[:2]


def shards(grad_out, act_in, basis_out, basis_in, eigen_vals, query_out, query_in):
    yi, zi, ci, li = (lax.axis_index(a) for a in ("y", "zh", "c", "zl"))
    tokens, unit = grad_out.shape[1:]
    queries, rank = query_out.shape[:2]
    rows = queries * rank
    half_rows = rows // 2
    width = basis_out.shape[1]
    first = ci == 0

    same = li == zi % 2
    xi = lax.axis_index("x")
    at = jnp.stack([yi, zi, ci, same, xi]).astype(jnp.int32)

    out_t = basis_out.T
    out_both = jnp.concatenate([out_t, shift(out_t, "c", 1)], 0)
    out_both = lax.optimization_barrier(out_both)
    eigen_other = shift(eigen_vals, "c", 1)
    inv0 = 1.0 / eigen_vals.astype(F32)
    inv1 = 1.0 / eigen_other.astype(F32)

    mine = lax.dynamic_slice_in_dim(query_out.reshape(rows, unit), ci * half_rows, half_rows, 0)
    mine_in = lax.dynamic_slice_in_dim(query_in.reshape(rows, -1), ci * half_rows, half_rows, 0)
    in_own = jnp.stack(gather(basis_in, "zh"))
    in_other = shift(in_own, "c", 1)
    *parts, value = rotate_in(at, gather(act_in[0], "y"), mine_in, (in_own, in_other))
    part = parts[0].astype(F32)
    for by in (1, 2, 3):
        part = part + shift(parts[by], "x", by).astype(F32)
    part = part.astype(BF)
    part = (part.astype(F32) + to_owner(part).astype(F32)).astype(BF)
    plus, far, minus = (from_owner(part, by) for by in (1, 2, 3))

    query = dot_t(mine, out_both).astype(BF)
    query = jnp.concatenate([query, value], 1)
    some = half_rows // 8
    query = exchange(query.reshape(8, some, -1), ("zl", "x")).reshape(8, some, -1)
    query = query.astype(F32).sum(0).astype(BF)
    query = spread(query, ("zl", "x"), 8).reshape(half_rows, -1)
    value = query[:, 2 * width :]
    query = query[:, : 2 * width]
    swapped = jnp.concatenate([query[:, width:], query[:, :width]], 1)
    query = jnp.concatenate([query, shift(swapped, "c", 1)], 0)
    query_rot = query.astype(F32).T

    act_rot = jnp.concatenate(
        [jnp.where(same, part, minus), jnp.where(same, far, plus), value], 0
    )
    act_rot = gather(act_rot, "y")
    value_other = shift(pick(act_rot, half_rows), "c", 1)

    grad = grad_out[0]
    plus, far, minus = (shift(grad, "zh", -by) for by in (1, 2, 3))
    blocks = []
    for some_blocks in ((grad,), (plus, minus), (far,)):
        some_blocks = jnp.stack(some_blocks)
        found = lax.all_gather(some_blocks, "y", axis=0, tiled=True)
        product = dot_t(found.reshape(-1, unit), out_both).astype(BF)
        product = product.reshape(4, -1, tokens, 2 * width)
        parts = [product]
        for by in (1, 2, 3):
            part = lax.dynamic_index_in_dim(product, (xi + by) % 4, 0, False)
            parts.append(shift(part, "x", by))
        blocks.append(parts)
    keeps, gots = [], []
    for a, b in (((blocks[0], 0), (blocks[1], 1)), ((blocks[2], 0), (blocks[1], 0))):
        keep, give = split(at, a, b)
        keeps.append(keep)
        gots.append(shift(give, "zl", 1))
    result = score(at, (*keeps, *gots), act_rot, value_other, inv0, inv1, query_rot)
    low = jnp.where(same, zi, (zi + 3) % 4) // 2

    result = result.reshape(2, queries, rank).sum(-1)
    result = jnp.where(low == 0, result, result[::-1])
    turned = jnp.concatenate([result[:, queries // 2 :], result[:, : queries // 2]], 1)
    result = jnp.where(first, result, turned)
    result = spread(result, ("y", "zh"), 16).reshape(16, 2, queries).sum(0)
    result = spread(result, ("c", "zl", "x"), 16).reshape(2, 2, 4, 2, queries)
    result = result.transpose(2, 3, 1, 0, 4).reshape(8, 4, queries)
    return lax.dynamic_index_in_dim(result, li * 4 + lax.axis_index("x"), 0, False)


def solution(mesh):
    fine = Mesh(mesh.devices.reshape(SIZES), AXES)
    dp, factor = ("y", "zh", "c"), ("zl", "x")
    in_specs = (
        P(dp, None, factor),
        P(dp, None, factor),
        P(factor, dp),
        P(factor, dp),
        P(dp, None),
        P(None, None, factor),
        P(None, None, factor),
    )

    return jax.shard_map(
        shards, mesh=fine, in_specs=in_specs, out_specs=P(factor, None), check_vma=False
    )
```
